32 devices in a mesh: blk: 2 (over x), rows: 16 (over z, y, core).
Axes of the slice: x: 2, y: 2, z: 4, core: 2. Of those that a mesh axis runs over, the one named last changes fastest.
Arguments:
- snapshots: float32 [32768, 512], P('rows', 'blk'), may hold values from -40 to 40
- grades: int32 [512], P('blk'), may hold values from 0 to 7
- mover: int32 [3, 2], P(None, 'blk'), may hold values from 0 to 1
Outputs:
- basis: float32 [32768, 512], P('rows', 'blk')
The draws below stay inside these ranges and needn't reach their ends.
All inputs are finite; a program needn't handle non-finite values.
Results may differ from the reference program's by a relative error of at most 0.0001.
Values sent between devices are 32-bit elements; how exact they have to be, the bound alone decides.
A program may use at most 64 MiB of HBM per device.

```python
import math
import jax
import jax.numpy as jnp
from jax import lax

BW = 128
ROUNDS = 4
NS_STEPS = 3
GRADES = 8
ROWS = 32768
COLS = 512
N_BLK = 2


factor_count = 32


def draw_snapshots(key, part):
    keys = jax.random.split(jax.random.fold_in(key, 11), 4)
    noise = jnp.clip(jax.random.normal(keys[0], (ROWS, COLS), jnp.float32), -6.0, 6.0)
    latent = jnp.clip(jax.random.normal(keys[1], (ROWS, factor_count), jnp.float32), -4.0, 4.0)
    decay = 0.04 * jnp.power(0.9, jnp.arange(factor_count, dtype=jnp.float32))
    loading = jax.random.uniform(keys[2], (factor_count, COLS), jnp.float32, -1.0, 1.0) * decay[:, None]
    common = jnp.dot(latent, loading, precision=jax.lax.Precision.HIGHEST)
    column_scale = jnp.exp(jax.random.uniform(keys[3], (1, COLS), jnp.float32, math.log(0.3), math.log(3.0)))
    values = (noise + common) * column_scale
    return jnp.clip(values, -40.0, 40.0)


def with_ends(entries, rng, least, top_value):
    extent = entries.shape
    index_at = [jax.random.randint(jax.random.fold_in(rng, axis), (), 0, extent[axis]) for axis in range(len(extent))]
    entries = entries.at[tuple(index_at)].set(least)
    longest = extent.index(max(extent))
    index_at[longest] = (index_at[longest] + 1) % extent[longest]
    return entries.at[tuple(index_at)].set(top_value)


def setup_inputs(seed: int = 0) -> dict:
    streams_of = jax.random.split(jax.random.key(seed), 4)
    return {
        "snapshots": draw_snapshots(jax.random.fold_in(streams_of[3], 71), 0),
        "grades": with_ends(jax.random.randint(streams_of[1], (COLS,), 0, GRADES), jax.random.fold_in(streams_of[1], 1), 0, GRADES - 1).astype(jnp.int32),
        "mover": with_ends(jax.random.randint(streams_of[2], (ROUNDS - 1, N_BLK), 0, 2), jax.random.fold_in(streams_of[2], 1), 0, 1).astype(jnp.int32),
    }


epsilon = 1e-06
relaxation = 1.2

def rotation(cross_gram, squares, labels):
    left_scale = lax.rsqrt(squares[:BW] + epsilon)
    right_scale = lax.rsqrt(squares[BW:] + epsilon)
    grade_gap = jnp.abs(labels[:BW, None] - labels[None, BW:])
    scaled = cross_gram * left_scale[:, None] * right_scale[None, :] / (1.0 + grade_gap)
    magnitude = jnp.sqrt(jnp.sum(scaled * scaled) + epsilon)
    generator = relaxation * scaled / magnitude
    zeros_block = jnp.zeros_like(generator)
    upper_half = jnp.concatenate([zeros_block, generator], 1)
    lower_half = jnp.concatenate([-generator.T, zeros_block], 1)
    iterate = jnp.eye(2 * BW, dtype=generator.dtype) + jnp.concatenate([upper_half, lower_half], 0)
    for sweep in range(NS_STEPS):
        product = lax.dot_general(iterate, iterate, (((0,), (0,)), ((), ())), precision=lax.Precision.HIGHEST)
        iterate = 1.5 * iterate - 0.5 * jnp.dot(iterate, product, precision=lax.Precision.HIGHEST)
    return iterate

def reference(snapshots, grades, mover):
    blocks = snapshots.reshape(ROWS, N_BLK, 2 * BW)
    labels = grades.reshape(N_BLK, 2 * BW).astype(snapshots.dtype)
    for round_index in range(ROUNDS):
        cross_gram = jnp.einsum('mpi,mpj->pij', blocks[:, :, :BW], blocks[:, :, BW:], precision=lax.Precision.HIGHEST)
        squares = lax.optimization_barrier(jnp.sum(blocks * blocks, axis=0))
        rotator = jax.vmap(rotation)(cross_gram, squares, labels)
        blocks = jnp.einsum('mpi,pij->mpj', blocks, rotator, precision=lax.Precision.HIGHEST)
        if round_index + 1 < ROUNDS:
            first = mover[round_index] == 0
            first_blocks = first[None, :, None]
            first_labels = first[:, None]
            moving = jnp.where(first_blocks, blocks[:, :, :BW], blocks[:, :, BW:])
            staying = jnp.where(first_blocks, blocks[:, :, BW:], blocks[:, :, :BW])
            move_label = jnp.where(first_labels, labels[:, :BW], labels[:, BW:])
            stay_label = jnp.where(first_labels, labels[:, BW:], labels[:, :BW])
            moving = jnp.roll(moving, 1, axis=1)
            move_label = jnp.roll(move_label, 1, axis=0)
            blocks = jnp.where(first_blocks, jnp.concatenate([moving, staying], 2), jnp.concatenate([staying, moving], 2))
            labels = jnp.where(first_labels, jnp.concatenate([move_label, stay_label], 1), jnp.concatenate([stay_label, move_label], 1))
    return blocks.reshape(ROWS, COLS)
```

```python
import functools

import jax
import jax.numpy as jnp
from jax import lax
from jax.experimental import pallas as pl
from jax.experimental.pallas import tpu as pltpu
from jax.sharding import PartitionSpec as P

BW = 128
ROUNDS = 4
NS_STEPS = 3
CHUNKS = 4

epsilon = 1e-06
relaxation = 1.2

MESH = pl.DeviceIdType.MESH
ROWS_DIM = (((0,), (0,)), ((), ()))
PLAIN = (((1,), (0,)), ((), ()))
VMEM = pl.BlockSpec(memory_space=pltpu.VMEM)
ANY = pl.BlockSpec(memory_space=pl.ANY)


def from_behind(value, axis, by):
    peers = lax.axis_size(axis)
    return lax.ppermute(value, axis, [(i, (i + by) % peers) for i in range(peers)])


def rotation(cross_gram, squares, labels):
    left_scale = lax.rsqrt(squares[:BW] + epsilon)
    right_scale = lax.rsqrt(squares[BW:] + epsilon)
    grade_gap = jnp.abs(labels[:BW, None] - labels[None, BW:])
    scaled = cross_gram * left_scale[:, None] * right_scale[None, :] / (1.0 + grade_gap)
    magnitude = jnp.sqrt(jnp.sum(scaled * scaled) + epsilon)
    generator = relaxation * scaled / magnitude
    zeros_block = jnp.zeros_like(generator)
    upper_half = jnp.concatenate([zeros_block, generator], 1)
    lower_half = jnp.concatenate([-generator.T, zeros_block], 1)
    iterate = jnp.eye(2 * BW, dtype=generator.dtype) + jnp.concatenate([upper_half, lower_half], 0)
    for sweep in range(NS_STEPS):
        product = lax.dot_general(iterate, iterate, ROWS_DIM, precision=lax.Precision.HIGHEST)
        iterate = 1.5 * iterate - 0.5 * jnp.dot(iterate, product, precision=lax.Precision.HIGHEST)
    return iterate


def statistics(blocks):
    cross_part = lax.dot_general(
        blocks[:, :BW], blocks[:, BW:], ROWS_DIM, precision=lax.Precision.HIGHEST
    )
    square_part = jnp.sum(blocks * blocks, axis=0)
    return lax.psum((cross_part, square_part), "rows")


def assemble(first, incoming, staying):
    return jnp.where(
        first, jnp.concatenate([incoming, staying], -1), jnp.concatenate([staying, incoming], -1)
    )


def general_body(snapshots, grades, mover):
    blocks = snapshots
    labels = grades.astype(jnp.float32)
    for round_index in range(ROUNDS):
        cross_gram, squares = statistics(blocks)
        rotator = rotation(cross_gram, squares, labels)
        blocks = jnp.dot(blocks, rotator, precision=lax.Precision.HIGHEST)
        if round_index + 1 < ROUNDS:
            first = mover[round_index, 0] == 0
            move_label = jnp.where(first, labels[:BW], labels[BW:])
            stay_label = jnp.where(first, labels[BW:], labels[:BW])
            moving = jnp.where(first, blocks[:, :BW], blocks[:, BW:])
            staying = jnp.where(first, blocks[:, BW:], blocks[:, :BW])
            incoming, came_label = from_behind((moving, move_label), "blk", 1)
            blocks = assemble(first, incoming, staying)
            labels = assemble(first, came_label, stay_label)
    return blocks


def split(value):
    high = value.astype(jnp.bfloat16)
    return high, (value - high.astype(jnp.float32)).astype(jnp.bfloat16)


def dot_split(a, b, dims=PLAIN):
    (ah, al), (bh, bl) = a, b
    mul = functools.partial(lax.dot_general, dimension_numbers=dims, preferred_element_type=jnp.float32)
    return mul(ah, bh) + (mul(ah, bl) + mul(al, bh))


def dot3(a, b, dims=PLAIN):
    return dot_split(split(a), split(b), dims)


def dot6(a, b, dims=PLAIN):
    return lax.dot_general(
        a, b, dims, precision=lax.Precision.HIGHEST, preferred_element_type=jnp.float32
    )


def gram_kernel(
    n, x_ref, meta_ref, gram_ref, meta_out, half_ref,
    came, dpart, dgot, dfull, dother, cpart, cgot, cmine, cother, cfull, meta_got,
    x_send, x_recv, rs_send, rs_recv, ag_send, ag_recv, one_send, one_recv, local_sem,
):
    pos, me = lax.axis_index("blk"), lax.axis_index("rows")
    other = 1 - pos
    rows, width = x_ref.shape
    half = rows // 2
    piece = half // CHUNKS
    share = width // n
    partner = (other, me)

    barrier = pltpu.get_barrier_semaphore()
    for k in range(1, n):
        pl.semaphore_signal(
            barrier, inc=1, device_id=(pos, lax.rem(me + k, n)), device_id_type=MESH
        )
    pl.semaphore_signal(barrier, inc=1, device_id=partner, device_id_type=MESH)
    pl.semaphore_wait(barrier, n)

    def remote(src, dst, send, recv, device):
        return pltpu.make_async_remote_copy(
            src_ref=src, dst_ref=dst, send_sem=send, recv_sem=recv,
            device_id=device, device_id_type=MESH,
        )

    labels = remote(meta_ref, meta_got, one_send.at[0], one_recv.at[0], partner)
    labels.start()
    swaps = []
    for c in range(CHUNKS):
        source = x_ref.at[pl.ds(pl.multiple_of(other * half + c * piece, piece), piece)]
        swaps.append(
            remote(source, came.at[pl.ds(c * piece, piece)], x_send.at[c], x_recv.at[c], partner)
        )
        swaps[-1].start()

    def scatter(part, got, which):
        copies = []
        for k in range(1, n):
            peer = lax.rem(me + k, n)
            copies.append(
                remote(part.at[peer], got.at[k], rs_send.at[which, k], rs_recv.at[which, k], (pos, peer))
            )
            copies[-1].start()
        return copies

    def gather(full, which):
        copies = []
        for k in range(1, n):
            peer = lax.rem(me + k, n)
            copies.append(
                remote(full.at[me], full.at[me], ag_send.at[which, k], ag_recv.at[which, k], (pos, peer))
            )
            copies[-1].start()
        return copies

    def summed(part, got, copies):
        total = part[me]
        for k in range(1, n):
            copies[k - 1].wait()
            total = total + got[k]
        return total

    tile = piece
    own = jnp.zeros((width, width), jnp.float32)
    for t in range(rows // tile):
        block = split(x_ref[t * tile:(t + 1) * tile, :])
        own = own + dot_split(block, block, ROWS_DIM)
    dpart[...] = own.reshape(n, share, width)
    d_scatter = scatter(dpart, dgot, 0)

    def cross(c):
        swaps[c].wait()
        mine = x_ref[pl.ds(pl.multiple_of(pos * half + c * piece, piece), piece), :]
        theirs = came[c * piece:(c + 1) * piece, :]
        left = jnp.where(pos == 0, mine, theirs)
        right = jnp.where(pos == 0, theirs, mine)
        return dot3(left, right, ROWS_DIM)

    total = cross(0)
    dfull[me] = summed(dpart, dgot, d_scatter)
    d_gather = gather(dfull, 0)
    for c in range(1, CHUNKS - 1):
        total = total + cross(c)
    for copy in d_gather:
        copy.wait()
    d_swap = remote(dfull, dother, one_send.at[1], one_recv.at[1], partner)
    d_swap.start()
    total = total + cross(CHUNKS - 1)
    cpart[...] = total.reshape(n, share, width)
    c_scatter = scatter(cpart, cgot, 1)
    keep = pltpu.make_async_copy(came, half_ref, local_sem)
    keep.start()
    cmine[...] = summed(cpart, cgot, c_scatter)
    c_swap = remote(cmine, cother, one_send.at[2], one_recv.at[2], partner)
    c_swap.start()
    labels.wait()
    meta_out[pos] = meta_ref[...]
    meta_out[other] = meta_got[...]
    d_swap.wait()
    gram_ref[pos] = dfull[...].reshape(width, width)
    gram_ref[other] = dother[...].reshape(width, width)
    c_swap.wait()
    cfull[me] = cmine[...] + cother[...]
    c_gather = gather(cfull, 1)
    for copy in c_gather:
        copy.wait()
    gram_ref[2] = cfull[...].reshape(width, width)
    keep.wait()


def polar(cross_gram, left_square, right_square, left_label, right_label):
    left_scale = lax.rsqrt(left_square + epsilon)
    right_scale = lax.rsqrt(right_square + epsilon)
    scaled = cross_gram * left_scale * right_scale / (1.0 + jnp.abs(left_label - right_label))
    magnitude = jnp.sqrt(jnp.sum(scaled * scaled, keepdims=True) + epsilon)
    return relaxation * scaled / magnitude


def eye(n):
    return (
        lax.broadcasted_iota(jnp.int32, (n, n), 0) == lax.broadcasted_iota(jnp.int32, (n, n), 1)
    ).astype(jnp.float32)


def rotations(generators):
    unit = eye(BW)
    signs = [split(b) for b in generators]
    turned = [split(b.T) for b in generators]
    norm = []
    for b, bt in zip(signs, turned):
        norm.append(unit + dot_split(b, bt))
        norm.append(unit + dot_split(bt, b))
    gain = None
    for sweep in range(NS_STEPS):
        factor = [1.5 * unit - 0.5 * v for v in norm]
        cut = [split(f) for f in factor]
        last = sweep + 1 == NS_STEPS
        if last:
            edge = [dot_split(cut[2 * i], split(e)) for i, e in enumerate(edge)]
        else:
            parts = [split(v) for v in norm]
            inner = [2.25 * unit - 1.5 * v + 0.25 * dot_split(p, p) for v, p in zip(norm, parts)]
            norm = [dot_split(p, split(v)) for p, v in zip(parts, inner)]
        if gain is None:
            gain = factor
        else:
            gain = [dot_split(split(g), f) for g, f in zip(gain, cut)]
        if sweep + 2 == NS_STEPS:
            edge = [dot_split(split(gain[2 * i]), b) for i, b in enumerate(signs)]
    out = []
    for i, e in enumerate(edge):
        upper = jnp.concatenate([gain[2 * i], e], 1)
        lower = jnp.concatenate([-e.T, gain[2 * i + 1]], 1)
        out.append(jnp.concatenate([upper, lower], 0))
    return out


def chain_kernel(gram_ref, meta_ref, own_ref, other_ref, g, w, lab):
    pos = lax.axis_index("blk")
    width = 2 * BW
    unit = eye(width)
    for i in range(4):
        p, s = divmod(i, 2)
        for j in range(4):
            q, t = divmod(j, 2)
            rows, cols = slice(s * BW, s * BW + BW), slice(t * BW, t * BW + BW)
            if p == q:
                g[4 * i + j] = gram_ref[p, rows, cols]
            elif p == 0:
                g[4 * i + j] = gram_ref[2, rows, cols]
                g[4 * j + i] = gram_ref[2, rows, cols].T
        lab[i] = jnp.broadcast_to(meta_ref[p, 0:1, s * BW:(s + 1) * BW], (BW, BW))
    small = eye(BW)
    slots = [[0, 1], [2, 3]]

    def generator(a, b):
        left_square = jnp.sum(g[4 * a + a] * small, axis=1, keepdims=True)
        right_square = jnp.sum(g[4 * b + b] * small, axis=0, keepdims=True)
        return polar(g[4 * a + b], left_square, right_square, lab[a].T, lab[b])

    def turn(a, b, q, r):
        if r == 0:
            p = a // 2
            w[a] = jnp.zeros((2 * width, BW), jnp.float32)
            w[b] = jnp.zeros((2 * width, BW), jnp.float32)
            w[a, p * width:(p + 1) * width] = q[:, :BW]
            w[b, p * width:(p + 1) * width] = q[:, BW:]
        else:
            both = dot3(jnp.concatenate([w[a], w[b]], 1), q)
            w[a] = both[:, :BW]
            w[b] = both[:, BW:]

    for r in range(ROUNDS - 1):
        qs = rotations([generator(*slots[p]) for p in range(2)])
        for p in range(2):
            turn(*slots[p], qs[p], r)
        for p, q in ((0, 0), (1, 1), (0, 1)):
            (a, b), (c, d) = slots[p], slots[q]
            upper = jnp.concatenate([g[4 * a + c], g[4 * a + d]], 1)
            lower = jnp.concatenate([g[4 * b + c], g[4 * b + d]], 1)
            block = jnp.concatenate([upper, lower], 0)
            block = dot6(qs[p], dot6(block, qs[q]), ROWS_DIM)
            for i, e in enumerate((a, b)):
                for j, f in enumerate((c, d)):
                    value = block[i * BW:(i + 1) * BW, j * BW:(j + 1) * BW]
                    g[4 * e + f] = value
                    if p != q:
                        g[4 * f + e] = value.T
        first = [jnp.max(meta_ref[p, r + 1:r + 2, :BW]) < 0.5 for p in range(2)]
        moving = [jnp.where(first[p], slots[p][0], slots[p][1]) for p in range(2)]
        staying = [jnp.where(first[p], slots[p][1], slots[p][0]) for p in range(2)]
        slots = [
            [
                jnp.where(first[p], moving[1 - p], staying[p]),
                jnp.where(first[p], staying[p], moving[1 - p]),
            ]
            for p in range(2)
        ]
    a = jnp.where(pos == 0, slots[0][0], slots[1][0])
    b = jnp.where(pos == 0, slots[0][1], slots[1][1])
    (q,) = rotations([generator(a, b)])
    turn(a, b, q, ROUNDS)
    mine = pl.ds(pl.multiple_of(pos * width, width), width)
    theirs = pl.ds(pl.multiple_of((1 - pos) * width, width), width)
    own_ref[:, :BW] = w[a, mine]
    own_ref[:, BW:] = w[b, mine]
    other_ref[:, :BW] = w[a, theirs]
    other_ref[:, BW:] = w[b, theirs]


def apply_kernel(where_ref, x_ref, near_ref, far_ref, own_ref, other_ref, out_ref):
    partner = jnp.where(pl.program_id(0) == 0, near_ref[...], far_ref[...])
    out_ref[...] = dot3(x_ref[...], own_ref[...]) + dot3(partner, other_ref[...])


def pair_body(n, snapshots, grades, mover):
    rows, width = snapshots.shape
    share = width // n
    half = rows // 2
    pos = lax.axis_index("blk")
    f32 = jnp.float32
    meta = jnp.concatenate(
        [
            grades.astype(f32)[None],
            jnp.broadcast_to(mover.astype(f32), (ROUNDS - 1, width)),
            jnp.zeros((8 - ROUNDS, width), f32),
        ]
    )
    dma = pltpu.SemaphoreType.DMA
    shares = pltpu.VMEM((n, share, width), f32)
    gram, metas, near = pl.pallas_call(
        functools.partial(gram_kernel, n),
        out_shape=(
            jax.ShapeDtypeStruct((3, width, width), f32),
            jax.ShapeDtypeStruct((2, 8, width), f32),
            jax.ShapeDtypeStruct((half, width), f32),
        ),
        in_specs=[VMEM, VMEM],
        out_specs=(VMEM, VMEM, ANY),
        scratch_shapes=[
            pltpu.VMEM((half, width), f32),
            shares, shares, shares, shares,
            shares, shares, pltpu.VMEM((share, width), f32), pltpu.VMEM((share, width), f32), shares,
            pltpu.VMEM((8, width), f32),
            dma((CHUNKS,)), dma((CHUNKS,)), dma((2, n)), dma((2, n)), dma((2, n)), dma((2, n)),
            dma((3,)), dma((3,)), dma,
        ],
        compiler_params=pltpu.CompilerParams(
            collective_id=0, has_side_effects=True, vmem_limit_bytes=40 * 1024 * 1024
        ),
    )(snapshots, meta)
    late = lax.dynamic_slice_in_dim(snapshots, pos * half, half, 0)
    late, gram = lax.optimization_barrier((late, gram))
    far = lax.ppermute(late, "blk", [(0, 1), (1, 0)])
    w_own, w_other = pl.pallas_call(
        chain_kernel,
        out_shape=(jax.ShapeDtypeStruct((width, width), f32),) * 2,
        in_specs=[VMEM, VMEM],
        out_specs=(VMEM, VMEM),
        scratch_shapes=[
            pltpu.VMEM((16, BW, BW), f32),
            pltpu.VMEM((4, 2 * width, BW), f32),
            pltpu.VMEM((4, BW, BW), f32),
        ],
        compiler_params=pltpu.CompilerParams(vmem_limit_bytes=40 * 1024 * 1024),
        cost_estimate=pl.CostEstimate(
            flops=20 * 10**9, bytes_accessed=4 * width * width * 6, transcendentals=0
        ),
    )(gram, metas)
    tile = half // CHUNKS
    out = pl.pallas_call(
        apply_kernel,
        out_shape=jax.ShapeDtypeStruct((rows, width), f32),
        grid_spec=pltpu.PrefetchScalarGridSpec(
            num_scalar_prefetch=1,
            grid=(2, CHUNKS),
            in_specs=[
                pl.BlockSpec((tile, width), lambda j, i, s: (lax.rem(s[0] + j, 2) * CHUNKS + i, 0)),
                pl.BlockSpec((tile, width), lambda j, i, s: (jnp.where(j == 0, i, CHUNKS - 1), 0)),
                pl.BlockSpec((tile, width), lambda j, i, s: (jnp.where(j == 0, 0, i), 0)),
                pl.BlockSpec((width, width), lambda j, i, s: (0, 0)),
                pl.BlockSpec((width, width), lambda j, i, s: (0, 0)),
            ],
            out_specs=pl.BlockSpec((tile, width), lambda j, i, s: (lax.rem(s[0] + j, 2) * CHUNKS + i, 0)),
        ),
    )(jnp.asarray(pos, jnp.int32).reshape(1), snapshots, near, far, w_own, w_other)
    return out


def solution(mesh):
    placed = (P("rows", "blk"), P("blk"), P(None, "blk"))
    n = mesh.shape["rows"]
    pairs = mesh.shape["blk"] == 2 and (2 * BW) % (8 * n) == 0
    body = functools.partial(pair_body, n) if pairs else general_body
    return jax.shard_map(
        body, mesh=mesh, in_specs=placed, out_specs=P("rows", "blk"), check_vma=False
    )
```

```python
import functools

import jax
import jax.numpy as jnp
from jax import lax
from jax.experimental import pallas as pl
from jax.experimental.pallas import tpu as pltpu
from jax.sharding import PartitionSpec as P

BW = 128
ROUNDS = 4
NS_STEPS = 3
CHUNKS = 4
EXTRA = 1

epsilon = 1e-06
relaxation = 1.2

MESH = pl.DeviceIdType.MESH
ROWS_DIM = (((0,), (0,)), ((), ()))
PLAIN = (((1,), (0,)), ((), ()))
VMEM = pl.BlockSpec(memory_space=pltpu.VMEM)
ANY = pl.BlockSpec(memory_space=pl.ANY)


def from_behind(value, axis, by):
    peers = lax.axis_size(axis)
    return lax.ppermute(value, axis, [(i, (i + by) % peers) for i in range(peers)])


def rotation(cross_gram, squares, labels):
    left_scale = lax.rsqrt(squares[:BW] + epsilon)
    right_scale = lax.rsqrt(squares[BW:] + epsilon)
    grade_gap = jnp.abs(labels[:BW, None] - labels[None, BW:])
    scaled = cross_gram * left_scale[:, None] * right_scale[None, :] / (1.0 + grade_gap)
    magnitude = jnp.sqrt(jnp.sum(scaled * scaled) + epsilon)
    generator = relaxation * scaled / magnitude
    zeros_block = jnp.zeros_like(generator)
    upper_half = jnp.concatenate([zeros_block, generator], 1)
    lower_half = jnp.concatenate([-generator.T, zeros_block], 1)
    iterate = jnp.eye(2 * BW, dtype=generator.dtype) + jnp.concatenate([upper_half, lower_half], 0)
    for sweep in range(NS_STEPS):
        product = lax.dot_general(iterate, iterate, ROWS_DIM, precision=lax.Precision.HIGHEST)
        iterate = 1.5 * iterate - 0.5 * jnp.dot(iterate, product, precision=lax.Precision.HIGHEST)
    return iterate


def statistics(blocks):
    cross_part = lax.dot_general(
        blocks[:, :BW], blocks[:, BW:], ROWS_DIM, precision=lax.Precision.HIGHEST
    )
    square_part = jnp.sum(blocks * blocks, axis=0)
    return lax.psum((cross_part, square_part), "rows")


def assemble(first, incoming, staying):
    return jnp.where(
        first, jnp.concatenate([incoming, staying], -1), jnp.concatenate([staying, incoming], -1)
    )


def general_body(snapshots, grades, mover):
    blocks = snapshots
    labels = grades.astype(jnp.float32)
    for round_index in range(ROUNDS):
        cross_gram, squares = statistics(blocks)
        rotator = rotation(cross_gram, squares, labels)
        blocks = jnp.dot(blocks, rotator, precision=lax.Precision.HIGHEST)
        if round_index + 1 < ROUNDS:
            first = mover[round_index, 0] == 0
            move_label = jnp.where(first, labels[:BW], labels[BW:])
            stay_label = jnp.where(first, labels[BW:], labels[:BW])
            moving = jnp.where(first, blocks[:, :BW], blocks[:, BW:])
            staying = jnp.where(first, blocks[:, BW:], blocks[:, :BW])
            incoming, came_label = from_behind((moving, move_label), "blk", 1)
            blocks = assemble(first, incoming, staying)
            labels = assemble(first, came_label, stay_label)
    return blocks


def split(value):
    high = value.astype(jnp.bfloat16)
    return high, (value - high.astype(jnp.float32)).astype(jnp.bfloat16)


def dot_split(a, b, dims=PLAIN):
    (ah, al), (bh, bl) = a, b
    mul = functools.partial(lax.dot_general, dimension_numbers=dims, preferred_element_type=jnp.float32)
    return mul(ah, bh) + (mul(ah, bl) + mul(al, bh))


def dot3(a, b, dims=PLAIN):
    return dot_split(split(a), split(b), dims)


def dot6(a, b, dims=PLAIN):
    return lax.dot_general(
        a, b, dims, precision=lax.Precision.HIGHEST, preferred_element_type=jnp.float32
    )


def gram_kernel(
    n, x_ref, grade_ref, mover_ref, diag_ref, cross_ref, turn_ref, meta_out, near_ref,
    came, meta, meta_got, dpart, dgot, dmid, dnear, dfull, dother,
    cpart, cgot, cmid, cnear, cmine, cother, cfull,
    x_send, x_recv, rs_send, rs_recv, ag_send, ag_recv, sib_send, sib_recv, one_send, one_recv,
    local_sem,
):
    pos, me = lax.axis_index("blk"), lax.axis_index("rows")
    other = 1 - pos
    core, group = lax.rem(me, 2), me // 2
    groups = n // 2
    rows, width = x_ref.shape
    half = rows // 2
    piece = half // CHUNKS
    share = width // n
    partner, sibling = (other, me), (pos, me + 1 - 2 * core)
    peers = [None] + [lax.rem(group + k, groups) for k in range(1, groups)]

    barrier = pltpu.get_barrier_semaphore()
    for peer in peers[1:]:
        pl.semaphore_signal(barrier, inc=1, device_id=(pos, 2 * peer + core), device_id_type=MESH)
    for device in (partner, sibling):
        pl.semaphore_signal(barrier, inc=1, device_id=device, device_id_type=MESH)
    meta[...] = jnp.zeros_like(meta)
    meta[0:1, :] = grade_ref[...].astype(jnp.float32)
    for r in range(ROUNDS - 1):
        meta[r + 1:r + 2, :] = jnp.full((1, width), mover_ref[r, 0], jnp.int32).astype(jnp.float32)
    pl.semaphore_wait(barrier, groups + 1)

    def remote(src, dst, send, recv, device):
        copy = pltpu.make_async_remote_copy(
            src_ref=src, dst_ref=dst, send_sem=send, recv_sem=recv,
            device_id=device, device_id_type=MESH,
        )
        copy.start()
        return copy

    def swap(c):
        start = lax.rem(other * half + c * piece, rows)
        source = x_ref.at[pl.ds(pl.multiple_of(start, piece), piece)]
        return remote(source, came.at[pl.ds(c * piece, piece)], x_send.at[c], x_recv.at[c], partner)

    labels = remote(meta, meta_got, one_send.at[0], one_recv.at[0], partner)
    swaps = [swap(c) for c in range(CHUNKS)]

    def pair_up(part, got, which):
        return remote(part.at[1 - core], got, sib_send.at[which], sib_recv.at[which], sibling)

    def scatter(mid, near, which):
        return [
            remote(
                mid.at[peers[k]], near.at[k], rs_send.at[which, k], rs_recv.at[which, k],
                (pos, 2 * peers[k] + core),
            )
            for k in range(1, groups)
        ]

    def summed(mid, near, copies):
        total = mid[group]
        for k in range(1, groups):
            copies[k - 1].wait()
            total = total + near[k]
        return total

    def gather(full, which):
        return [
            remote(
                full.at[core, group], full.at[core, group], ag_send.at[which, k],
                ag_recv.at[which, k], (pos, 2 * peers[k] + core),
            )
            for k in range(1, groups)
        ]

    def hand_over(full, copies, which):
        for copy in copies:
            copy.wait()
        return remote(full.at[core], full.at[core], sib_send.at[which], sib_recv.at[which], sibling)

    def cross(c):
        swaps[c].wait()
        mine = x_ref[pl.ds(pl.multiple_of(pos * half + c * piece, piece), piece), :]
        theirs = came[c * piece:(c + 1) * piece, :]
        left = jnp.where(pos == 0, mine, theirs)
        right = jnp.where(pos == 0, theirs, mine)
        return dot3(left, right, ROWS_DIM)

    own = jnp.zeros((width, width), jnp.float32)
    for t in range(rows // piece):
        block = split(x_ref[t * piece:(t + 1) * piece, :])
        own = own + dot_split(block, block, ROWS_DIM)
    dpart[...] = own.reshape(2, groups, share, width)
    copy = pair_up(dpart, dgot, 0)
    total = cross(0)
    copy.wait()
    dmid[...] = dpart[core] + dgot[...]
    copies = scatter(dmid, dnear, 0)
    total = total + cross(1)
    dfull[core, group] = summed(dmid, dnear, copies)
    copies = gather(dfull, 0)
    total = total + cross(2)
    copy = hand_over(dfull, copies, 1)
    copy.wait()
    d_swap = remote(dfull, dother, one_send.at[1], one_recv.at[1], partner)
    for c in range(3, CHUNKS):
        total = total + cross(c)
    cpart[...] = total.reshape(2, groups, share, width)
    copy = pair_up(cpart, cgot, 2)
    copy.wait()
    cmid[...] = cpart[core] + cgot[...]
    copies = scatter(cmid, cnear, 1)
    cmine[...] = summed(cmid, cnear, copies)
    c_swap = remote(cmine, cother, one_send.at[2], one_recv.at[2], partner)
    late = [swap(c) for c in range(CHUNKS, CHUNKS + EXTRA)]
    c_swap.wait()
    cfull[core, group] = cmine[...] + cother[...]
    copies = gather(cfull, 1)

    labels.wait()
    meta_out[pos] = meta[...]
    meta_out[other] = meta_got[...]
    d_swap.wait()
    diag_ref[pos] = dfull[...].reshape(width, width)
    diag_ref[other] = dother[...].reshape(width, width)
    unit = eye(BW)
    generators = []
    for p in range(2):
        left_square = jnp.sum(diag_ref[p, :BW, :BW] * unit, axis=1, keepdims=True)
        right_square = jnp.sum(diag_ref[p, BW:, BW:] * unit, axis=0, keepdims=True)
        left_label = jnp.broadcast_to(meta_out[p, 0:1, :BW], (BW, BW)).T
        generators.append(
            polar(diag_ref[p, :BW, BW:], left_square, right_square, left_label, meta_out[p, 0:1, BW:])
        )
    for p, q in enumerate(rotations(generators)):
        turn_ref[p] = q
        diag_ref[p] = dot6(q, dot6(diag_ref[p], q), ROWS_DIM)

    copy = hand_over(cfull, copies, 3)
    copy.wait()
    cross_ref[...] = cfull[...].reshape(width, width)
    for copy in late:
        copy.wait()
    keep = pltpu.make_async_copy(came, near_ref, local_sem)
    keep.start()
    keep.wait()


def polar(cross_gram, left_square, right_square, left_label, right_label):
    left_scale = lax.rsqrt(left_square + epsilon)
    right_scale = lax.rsqrt(right_square + epsilon)
    scaled = cross_gram * left_scale * right_scale / (1.0 + jnp.abs(left_label - right_label))
    magnitude = jnp.sqrt(jnp.sum(scaled * scaled, keepdims=True) + epsilon)
    return relaxation * scaled / magnitude


def eye(n):
    return (
        lax.broadcasted_iota(jnp.int32, (n, n), 0) == lax.broadcasted_iota(jnp.int32, (n, n), 1)
    ).astype(jnp.float32)


def rotations(generators):
    unit = eye(BW)
    signs = [split(b) for b in generators]
    turned = [split(b.T) for b in generators]
    norm = []
    for b, bt in zip(signs, turned):
        norm.append(unit + dot_split(b, bt))
        norm.append(unit + dot_split(bt, b))
    gain = None
    for sweep in range(NS_STEPS):
        factor = [1.5 * unit - 0.5 * v for v in norm]
        cut = [split(f) for f in factor]
        last = sweep + 1 == NS_STEPS
        if last:
            edge = [dot_split(cut[2 * i], split(e)) for i, e in enumerate(edge)]
        else:
            parts = [split(v) for v in norm]
            inner = [2.25 * unit - 1.5 * v + 0.25 * dot_split(p, p) for v, p in zip(norm, parts)]
            norm = [dot_split(p, split(v)) for p, v in zip(parts, inner)]
        if gain is None:
            gain = factor
        else:
            gain = [dot_split(split(g), f) for g, f in zip(gain, cut)]
        if sweep + 2 == NS_STEPS:
            edge = [dot_split(split(gain[2 * i]), b) for i, b in enumerate(signs)]
    out = []
    for i, e in enumerate(edge):
        upper = jnp.concatenate([gain[2 * i], e], 1)
        lower = jnp.concatenate([-e.T, gain[2 * i + 1]], 1)
        out.append(jnp.concatenate([upper, lower], 0))
    return out


def chain_kernel(diag_ref, cross_ref, turn_ref, meta_ref, high_ref, low_ref, g, w, lab):
    pos = lax.axis_index("blk")
    width = 2 * BW
    small = eye(BW)
    between = dot6(turn_ref[0], dot6(cross_ref[...], turn_ref[1]), ROWS_DIM)
    for i in range(4):
        p, s = divmod(i, 2)
        rows = slice(s * BW, s * BW + BW)
        for j in range(4):
            q, t = divmod(j, 2)
            cols = slice(t * BW, t * BW + BW)
            if p == q:
                g[4 * i + j] = diag_ref[p, rows, cols]
            elif p == 0:
                g[4 * i + j] = between[rows, cols]
                g[4 * j + i] = between[rows, cols].T
        lab[i] = jnp.broadcast_to(meta_ref[p, 0:1, rows], (BW, BW))
        w[i] = jnp.zeros((2 * width, BW), jnp.float32)
        w[i, p * width:(p + 1) * width] = turn_ref[p, :, rows]

    def generator(a, b):
        left_square = jnp.sum(g[4 * a + a] * small, axis=1, keepdims=True)
        right_square = jnp.sum(g[4 * b + b] * small, axis=0, keepdims=True)
        return polar(g[4 * a + b], left_square, right_square, lab[a].T, lab[b])

    def step(slots, r):
        first = [jnp.max(meta_ref[p, r + 1:r + 2, :BW]) < 0.5 for p in range(2)]
        moving = [jnp.where(first[p], slots[p][0], slots[p][1]) for p in range(2)]
        staying = [jnp.where(first[p], slots[p][1], slots[p][0]) for p in range(2)]
        return [
            [
                jnp.where(first[p], moving[1 - p], staying[p]),
                jnp.where(first[p], staying[p], moving[1 - p]),
            ]
            for p in range(2)
        ]

    slots = step([[0, 1], [2, 3]], 0)
    for r in range(1, ROUNDS - 1):
        qs = rotations([generator(*slots[p]) for p in range(2)])
        for p, q in ((0, 0), (1, 1), (0, 1)):
            (a, b), (c, d) = slots[p], slots[q]
            upper = jnp.concatenate([g[4 * a + c], g[4 * a + d]], 1)
            lower = jnp.concatenate([g[4 * b + c], g[4 * b + d]], 1)
            block = jnp.concatenate([upper, lower], 0)
            block = dot6(qs[p], dot6(block, qs[q]), ROWS_DIM)
            for i, e in enumerate((a, b)):
                for j, f in enumerate((c, d)):
                    value = block[i * BW:(i + 1) * BW, j * BW:(j + 1) * BW]
                    g[4 * e + f] = value
                    if p != q:
                        g[4 * f + e] = value.T
        for p in range(2):
            a, b = slots[p]
            both = dot3(jnp.concatenate([w[a], w[b]], 1), qs[p])
            w[a] = both[:, :BW]
            w[b] = both[:, BW:]
        slots = step(slots, r)
    a = jnp.where(pos == 0, slots[0][0], slots[1][0])
    b = jnp.where(pos == 0, slots[0][1], slots[1][1])
    (q,) = rotations([generator(a, b)])
    cut = split(q)
    for p in range(2):
        rows = pl.ds(pl.multiple_of((pos if p == 0 else 1 - pos) * width, width), width)
        high, low = split(dot_split(split(jnp.concatenate([w[a, rows], w[b, rows]], 1)), cut))
        high_ref[p * width:(p + 1) * width] = high
        low_ref[p * width:(p + 1) * width] = low


def apply_kernel(first, count, tile, x_ref, partner_ref, high_ref, low_ref, *rest):
    out_ref, held, sems = rest[-3:]
    rows = x_ref.shape[0]
    blocks = rows // tile
    pos = lax.axis_index("blk")
    copies = []
    for i in range(count):
        there = pl.multiple_of(lax.rem(pos * CHUNKS + first + i, blocks) * tile, tile)
        here = slice(i * tile, i * tile + tile)
        data = split(jnp.concatenate([x_ref[pl.ds(there, tile), :], partner_ref[here, :]], 1))
        held[here, :] = dot_split(data, (high_ref[...], low_ref[...]))
        copies.append(
            pltpu.make_async_copy(held.at[here], out_ref.at[pl.ds(there, tile)], sems.at[i])
        )
        copies[-1].start()
    for copy in copies:
        copy.wait()


def apply(first, count, tile, snapshots, partner, high, low, out=None):
    rows, width = snapshots.shape
    extra = () if out is None else (out,)
    return pl.pallas_call(
        functools.partial(apply_kernel, first, count, tile),
        out_shape=jax.ShapeDtypeStruct((rows, width), jnp.float32),
        in_specs=[VMEM] * 4 + [ANY] * len(extra),
        out_specs=ANY,
        scratch_shapes=[
            pltpu.VMEM((count * tile, width), jnp.float32), pltpu.SemaphoreType.DMA((count,)),
        ],
        input_output_aliases={} if out is None else {4: 0},
        compiler_params=pltpu.CompilerParams(vmem_limit_bytes=24 * 1024 * 1024),
        cost_estimate=pl.CostEstimate(
            flops=count * tile * width * width * 48, bytes_accessed=count * tile * width * 16,
            transcendentals=0,
        ),
    )(snapshots, partner, high, low, *extra)


def pair_body(n, snapshots, grades, mover):
    rows, width = snapshots.shape
    share = width // n
    half = rows // 2
    tile = half // CHUNKS
    early = half + EXTRA * tile
    pos = lax.axis_index("blk")
    f32 = jnp.float32
    dma = pltpu.SemaphoreType.DMA
    whole = pltpu.VMEM((2, n // 2, share, width), f32)
    part = pltpu.VMEM((n // 2, share, width), f32)
    one = pltpu.VMEM((share, width), f32)
    square = jax.ShapeDtypeStruct((width, width), f32)
    squares = jax.ShapeDtypeStruct((2, width, width), f32)
    diag, cross, turn, meta, near = pl.pallas_call(
        functools.partial(gram_kernel, n),
        out_shape=(
            squares, square, squares,
            jax.ShapeDtypeStruct((2, 8, width), f32),
            jax.ShapeDtypeStruct((early, width), f32),
        ),
        in_specs=[VMEM, VMEM, pl.BlockSpec(memory_space=pltpu.SMEM)],
        out_specs=(VMEM, VMEM, VMEM, VMEM, ANY),
        scratch_shapes=[
            pltpu.VMEM((early, width), f32), pltpu.VMEM((8, width), f32), pltpu.VMEM((8, width), f32),
            whole, part, part, part, whole, whole,
            whole, part, part, part, one, one, whole,
            dma((CHUNKS + EXTRA,)), dma((CHUNKS + EXTRA,)),
            dma((2, n // 2)), dma((2, n // 2)), dma((2, n // 2)), dma((2, n // 2)),
            dma((4,)), dma((4,)), dma((3,)), dma((3,)), dma,
        ],
        compiler_params=pltpu.CompilerParams(
            collective_id=0, has_side_effects=True, vmem_limit_bytes=40 * 1024 * 1024
        ),
    )(snapshots, grades.reshape(1, width), mover)
    late = lax.dynamic_slice_in_dim(snapshots, pos * half + EXTRA * tile, rows - early, 0)
    late, cross = lax.optimization_barrier((late, cross))
    far = lax.ppermute(late, "blk", [(0, 1), (1, 0)])
    high, low = pl.pallas_call(
        chain_kernel,
        out_shape=(jax.ShapeDtypeStruct((2 * width, width), jnp.bfloat16),) * 2,
        in_specs=[VMEM] * 4,
        out_specs=(VMEM, VMEM),
        scratch_shapes=[
            pltpu.VMEM((16, BW, BW), f32),
            pltpu.VMEM((4, 2 * width, BW), f32),
            pltpu.VMEM((4, BW, BW), f32),
        ],
        compiler_params=pltpu.CompilerParams(vmem_limit_bytes=32 * 1024 * 1024),
        cost_estimate=pl.CostEstimate(
            flops=15 * 10**9, bytes_accessed=4 * width * width * 8, transcendentals=0
        ),
    )(diag, cross, turn, meta)
    done = CHUNKS + EXTRA
    out = apply(0, done, tile, snapshots, near, high, low)
    return apply(done, CHUNKS - EXTRA, tile, snapshots, far, high, low, out)


def solution(mesh):
    placed = (P("rows", "blk"), P("blk"), P(None, "blk"))
    n = mesh.shape["rows"]
    pairs = mesh.shape["blk"] == 2 and n % 2 == 0 and (2 * BW) % (8 * n) == 0
    body = functools.partial(pair_body, n) if pairs else general_body
    return jax.shard_map(
        body, mesh=mesh, in_specs=placed, out_specs=P("rows", "blk"), check_vma=False
    )
```

```python
import functools

import jax
import jax.numpy as jnp
from jax import lax
from jax.experimental import pallas as pl
from jax.experimental.pallas import tpu as pltpu
from jax.sharding import PartitionSpec as P

BW = 128
ROUNDS = 4
NS_STEPS = 3
CHUNKS = 8
EXTRA = 4
SOON = 1
TALL = 2

epsilon = 1e-06
relaxation = 1.2

MESH = pl.DeviceIdType.MESH
ROWS_DIM = (((0,), (0,)), ((), ()))
PLAIN = (((1,), (0,)), ((), ()))
VMEM = pl.BlockSpec(memory_space=pltpu.VMEM)
ANY = pl.BlockSpec(memory_space=pl.ANY)
HBM = pl.BlockSpec(memory_space=pltpu.HBM)


def from_behind(value, axis, by):
    peers = lax.axis_size(axis)
    return lax.ppermute(value, axis, [(i, (i + by) % peers) for i in range(peers)])


def rotation(cross_gram, squares, labels):
    left_scale = lax.rsqrt(squares[:BW] + epsilon)
    right_scale = lax.rsqrt(squares[BW:] + epsilon)
    grade_gap = jnp.abs(labels[:BW, None] - labels[None, BW:])
    scaled = cross_gram * left_scale[:, None] * right_scale[None, :] / (1.0 + grade_gap)
    magnitude = jnp.sqrt(jnp.sum(scaled * scaled) + epsilon)
    generator = relaxation * scaled / magnitude
    zeros_block = jnp.zeros_like(generator)
    upper_half = jnp.concatenate([zeros_block, generator], 1)
    lower_half = jnp.concatenate([-generator.T, zeros_block], 1)
    iterate = jnp.eye(2 * BW, dtype=generator.dtype) + jnp.concatenate([upper_half, lower_half], 0)
    for sweep in range(NS_STEPS):
        product = lax.dot_general(iterate, iterate, ROWS_DIM, precision=lax.Precision.HIGHEST)
        iterate = 1.5 * iterate - 0.5 * jnp.dot(iterate, product, precision=lax.Precision.HIGHEST)
    return iterate


def statistics(blocks):
    cross_part = lax.dot_general(
        blocks[:, :BW], blocks[:, BW:], ROWS_DIM, precision=lax.Precision.HIGHEST
    )
    square_part = jnp.sum(blocks * blocks, axis=0)
    return lax.psum((cross_part, square_part), "rows")


def assemble(first, incoming, staying):
    return jnp.where(
        first, jnp.concatenate([incoming, staying], -1), jnp.concatenate([staying, incoming], -1)
    )


def general_body(snapshots, grades, mover):
    blocks = snapshots
    labels = grades.astype(jnp.float32)
    for round_index in range(ROUNDS):
        cross_gram, squares = statistics(blocks)
        rotator = rotation(cross_gram, squares, labels)
        blocks = jnp.dot(blocks, rotator, precision=lax.Precision.HIGHEST)
        if round_index + 1 < ROUNDS:
            first = mover[round_index, 0] == 0
            move_label = jnp.where(first, labels[:BW], labels[BW:])
            stay_label = jnp.where(first, labels[BW:], labels[:BW])
            moving = jnp.where(first, blocks[:, :BW], blocks[:, BW:])
            staying = jnp.where(first, blocks[:, BW:], blocks[:, :BW])
            incoming, came_label = from_behind((moving, move_label), "blk", 1)
            blocks = assemble(first, incoming, staying)
            labels = assemble(first, came_label, stay_label)
    return blocks


def split(value):
    high = value.astype(jnp.bfloat16)
    return high, (value - high.astype(jnp.float32)).astype(jnp.bfloat16)


def dot_split(a, b, dims=PLAIN):
    (ah, al), (bh, bl) = a, b
    mul = functools.partial(lax.dot_general, dimension_numbers=dims, preferred_element_type=jnp.float32)
    return mul(ah, bh) + (mul(ah, bl) + mul(al, bh))


def dot3(a, b, dims=PLAIN):
    return dot_split(split(a), split(b), dims)


def dot6(a, b, dims=PLAIN):
    return lax.dot_general(
        a, b, dims, precision=lax.Precision.HIGHEST, preferred_element_type=jnp.float32
    )


def gram_kernel(
    n, x_hbm, grade_ref, mover_ref, diag_ref, cross_ref, turn_ref, meta_out, near_ref, late_ref,
    x_ref, grade, came, meta, meta_got, dpart, dgot, dmid, dnear, dfull, dother,
    cpart, cgot, cmid, cnear, cmine, cother, cfull,
    x_send, x_recv, rs_send, rs_recv, ag_send, ag_recv, sib_send, sib_recv, one_send, one_recv,
    load_sem, near_sem, side_sem,
):
    pos, me = lax.axis_index("blk"), lax.axis_index("rows")
    other = 1 - pos
    core, group = lax.rem(me, 2), me // 2
    groups = n // 2
    rows, width = x_ref.shape
    half = rows // 2
    piece = half // CHUNKS
    share = width // n
    partner, sibling = (other, me), (pos, me + 1 - 2 * core)
    peers = [None] + [lax.rem(group + k, groups) for k in range(1, groups)]

    grade_load = pltpu.make_async_copy(grade_ref, grade, side_sem.at[0])
    grade_load.start()
    loads = []
    for t in range(rows // piece):
        at = pl.ds(t * piece, piece)
        loads.append(pltpu.make_async_copy(x_hbm.at[at], x_ref.at[at], load_sem.at[t]))
        loads[-1].start()

    barrier = pltpu.get_barrier_semaphore()
    for peer in peers[1:]:
        pl.semaphore_signal(barrier, inc=1, device_id=(pos, 2 * peer + core), device_id_type=MESH)
    for device in (partner, sibling):
        pl.semaphore_signal(barrier, inc=1, device_id=device, device_id_type=MESH)
    meta[...] = jnp.zeros_like(meta)
    grade_load.wait()
    meta[0:1, :] = grade[...].astype(jnp.float32)
    for r in range(ROUNDS - 1):
        meta[r + 1:r + 2, :] = jnp.full((1, width), mover_ref[r, 0], jnp.int32).astype(jnp.float32)
    pl.semaphore_wait(barrier, groups + 1)

    def remote(src, dst, send, recv, device):
        copy = pltpu.make_async_remote_copy(
            src_ref=src, dst_ref=dst, send_sem=send, recv_sem=recv,
            device_id=device, device_id_type=MESH,
        )
        copy.start()
        return copy

    def swap(c):
        start = lax.rem(other * half + c * piece, rows)
        source = x_hbm.at[pl.ds(pl.multiple_of(start, piece), piece)]
        return remote(source, came.at[pl.ds(c * piece, piece)], x_send.at[c], x_recv.at[c], partner)

    labels = remote(meta, meta_got, one_send.at[0], one_recv.at[0], partner)
    swaps = [swap(c) for c in range(CHUNKS)]

    def pair_up(part, got, which):
        return remote(part.at[1 - core], got, sib_send.at[which], sib_recv.at[which], sibling)

    def scatter(mid, near, which):
        return [
            remote(
                mid.at[peers[k]], near.at[k], rs_send.at[which, k], rs_recv.at[which, k],
                (pos, 2 * peers[k] + core),
            )
            for k in range(1, groups)
        ]

    def summed(mid, near, copies):
        total = mid[group]
        for k in range(1, groups):
            copies[k - 1].wait()
            total = total + near[k]
        return total

    def gather(full, which):
        return [
            remote(
                full.at[core, group], full.at[core, group], ag_send.at[which, k],
                ag_recv.at[which, k], (pos, 2 * peers[k] + core),
            )
            for k in range(1, groups)
        ]

    def hand_over(full, copies, which):
        for copy in copies:
            copy.wait()
        return remote(full.at[core], full.at[core], sib_send.at[which], sib_recv.at[which], sibling)

    kept = []

    def keep(c):
        at = pl.ds(c * piece, piece)
        kept.append(pltpu.make_async_copy(came.at[at], near_ref.at[at], near_sem.at[c]))
        kept[-1].start()

    def cross(c):
        swaps[c].wait()
        keep(c)
        mine = x_ref[pl.ds(pl.multiple_of(pos * half + c * piece, piece), piece), :]
        theirs = came[c * piece:(c + 1) * piece, :]
        left = jnp.where(pos == 0, mine, theirs)
        right = jnp.where(pos == 0, theirs, mine)
        return dot3(left, right, ROWS_DIM)

    own = jnp.zeros((width, width), jnp.float32)
    for t in range(rows // piece):
        loads[t].wait()
        block = split(x_ref[t * piece:(t + 1) * piece, :])
        own = own + dot_split(block, block, ROWS_DIM)
    dpart[...] = own.reshape(2, groups, share, width)
    copy = pair_up(dpart, dgot, 0)
    begin = pl.multiple_of(pos * half + EXTRA * piece, piece)
    aside = pltpu.make_async_copy(
        x_ref.at[pl.ds(begin, half - EXTRA * piece)], late_ref, side_sem.at[1]
    )
    aside.start()
    total = cross(0) + cross(1)
    copy.wait()
    dmid[...] = dpart[core] + dgot[...]
    copies = scatter(dmid, dnear, 0)
    total = total + cross(2)
    dfull[core, group] = summed(dmid, dnear, copies)
    copies = gather(dfull, 0)
    total = total + cross(3) + cross(4)
    copy = hand_over(dfull, copies, 1)
    copy.wait()
    d_swap = remote(dfull, dother, one_send.at[1], one_recv.at[1], partner)
    late = [swap(c) for c in range(CHUNKS, CHUNKS + SOON)]
    for c in range(5, CHUNKS):
        total = total + cross(c)
    cpart[...] = total.reshape(2, groups, share, width)
    copy = pair_up(cpart, cgot, 2)
    diag_ref[pos] = dfull[...].reshape(width, width)
    labels.wait()
    meta_out[pos] = meta[...]
    meta_out[other] = meta_got[...]
    copy.wait()
    cmid[...] = cpart[core] + cgot[...]
    copies = scatter(cmid, cnear, 1)
    unit = eye(BW)

    def begin_round(p):
        diag = diag_ref[p]
        left_square = jnp.sum(diag[:BW, :BW] * unit, axis=1, keepdims=True)
        right_square = jnp.sum(diag[BW:, BW:] * unit, axis=0, keepdims=True)
        left_label = jnp.broadcast_to(meta_out[p, 0:1, :BW], (BW, BW)).T
        (q,) = rotations(
            [polar(diag[:BW, BW:], left_square, right_square, left_label, meta_out[p, 0:1, BW:])]
        )
        turn_ref[p] = q
        diag_ref[p] = dot6(q, dot6(diag, q), ROWS_DIM)

    begin_round(pos)
    cmine[...] = summed(cmid, cnear, copies)
    c_swap = remote(cmine, cother, one_send.at[2], one_recv.at[2], partner)
    late += [swap(c) for c in range(CHUNKS + SOON, CHUNKS + EXTRA)]
    d_swap.wait()
    diag_ref[other] = dother[...].reshape(width, width)
    c_swap.wait()
    cfull[core, group] = cmine[...] + cother[...]
    copies = gather(cfull, 1)
    begin_round(other)
    copy = hand_over(cfull, copies, 3)
    for c in range(EXTRA):
        late[c].wait()
        keep(CHUNKS + c)
    copy.wait()
    cross_ref[...] = cfull[...].reshape(width, width)
    aside.wait()
    for copy in kept:
        copy.wait()


def polar(cross_gram, left_square, right_square, left_label, right_label):
    left_scale = lax.rsqrt(left_square + epsilon)
    right_scale = lax.rsqrt(right_square + epsilon)
    scaled = cross_gram * left_scale * right_scale / (1.0 + jnp.abs(left_label - right_label))
    magnitude = jnp.sqrt(jnp.sum(scaled * scaled, keepdims=True) + epsilon)
    return relaxation * scaled / magnitude


def eye(n):
    return (
        lax.broadcasted_iota(jnp.int32, (n, n), 0) == lax.broadcasted_iota(jnp.int32, (n, n), 1)
    ).astype(jnp.float32)


def rotations(generators):
    unit = eye(BW)
    signs = [split(b) for b in generators]
    turned = [split(b.T) for b in generators]
    norm = []
    for b, bt in zip(signs, turned):
        norm.append(unit + dot_split(b, bt))
        norm.append(unit + dot_split(bt, b))
    gain = None
    for sweep in range(NS_STEPS):
        factor = [1.5 * unit - 0.5 * v for v in norm]
        cut = [split(f) for f in factor]
        last = sweep + 1 == NS_STEPS
        if last:
            edge = [dot_split(cut[2 * i], split(e)) for i, e in enumerate(edge)]
        else:
            parts = [split(v) for v in norm]
            inner = [2.25 * unit - 1.5 * v + 0.25 * dot_split(p, p) for v, p in zip(norm, parts)]
            norm = [dot_split(p, split(v)) for p, v in zip(parts, inner)]
        if gain is None:
            gain = factor
        else:
            gain = [dot_split(split(g), f) for g, f in zip(gain, cut)]
        if sweep + 2 == NS_STEPS:
            edge = [dot_split(split(gain[2 * i]), b) for i, b in enumerate(signs)]
    out = []
    for i, e in enumerate(edge):
        upper = jnp.concatenate([gain[2 * i], e], 1)
        lower = jnp.concatenate([-e.T, gain[2 * i + 1]], 1)
        out.append(jnp.concatenate([upper, lower], 0))
    return out


def chain_kernel(diag_ref, cross_ref, turn_ref, meta_ref, high_ref, low_ref, g, w, lab, squares):
    pos = lax.axis_index("blk")
    width = 2 * BW
    small = eye(BW)
    between = dot6(turn_ref[0], dot6(cross_ref[...], turn_ref[1]), ROWS_DIM)
    for i in range(4):
        p, s = divmod(i, 2)
        rows = slice(s * BW, s * BW + BW)
        for j in range(4):
            q, t = divmod(j, 2)
            cols = slice(t * BW, t * BW + BW)
            if p == q:
                g[4 * i + j] = diag_ref[p, rows, cols]
            elif p == 0:
                g[4 * i + j] = between[rows, cols]
                g[4 * j + i] = between[rows, cols].T
        lab[i] = jnp.broadcast_to(meta_ref[p, 0:1, rows], (BW, BW))
        w[i] = jnp.zeros((2 * width, BW), jnp.float32)
        w[i, p * width:(p + 1) * width] = turn_ref[p, :, rows]

    def generator(a, b, known=False):
        if known:
            left_square = jnp.broadcast_to(squares[a, 0:1], (BW, BW)).T
            right_square = squares[b, 0:1]
        else:
            left_square = jnp.sum(g[4 * a + a] * small, axis=1, keepdims=True)
            right_square = jnp.sum(g[4 * b + b] * small, axis=0, keepdims=True)
        return polar(g[4 * a + b], left_square, right_square, lab[a].T, lab[b])

    def step(slots, r):
        first = [jnp.max(meta_ref[p, r + 1:r + 2, :BW]) < 0.5 for p in range(2)]
        moving = [jnp.where(first[p], slots[p][0], slots[p][1]) for p in range(2)]
        staying = [jnp.where(first[p], slots[p][1], slots[p][0]) for p in range(2)]
        return [
            [
                jnp.where(first[p], moving[1 - p], staying[p]),
                jnp.where(first[p], staying[p], moving[1 - p]),
            ]
            for p in range(2)
        ]

    slots = step([[0, 1], [2, 3]], 0)
    for r in range(1, ROUNDS - 1):
        qs = rotations([generator(*slots[p]) for p in range(2)])
        last = r + 2 == ROUNDS
        for p, q in ((0, 0), (1, 1), (0, 1)):
            (a, b), (c, d) = slots[p], slots[q]
            upper = jnp.concatenate([g[4 * a + c], g[4 * a + d]], 1)
            lower = jnp.concatenate([g[4 * b + c], g[4 * b + d]], 1)
            block = jnp.concatenate([upper, lower], 0)
            block = dot6(block, qs[q])
            if last and p == q:
                square = jnp.sum(qs[p] * block, axis=0, keepdims=True)
                squares[a] = jnp.broadcast_to(square[:, :BW], (8, BW))
                squares[b] = jnp.broadcast_to(square[:, BW:], (8, BW))
                continue
            block = dot6(qs[p], block, ROWS_DIM)
            for i, e in enumerate((a, b)):
                for j, f in enumerate((c, d)):
                    value = block[i * BW:(i + 1) * BW, j * BW:(j + 1) * BW]
                    g[4 * e + f] = value
                    if p != q:
                        g[4 * f + e] = value.T
        for p in range(2):
            a, b = slots[p]
            both = dot3(jnp.concatenate([w[a], w[b]], 1), qs[p])
            w[a] = both[:, :BW]
            w[b] = both[:, BW:]
        slots = step(slots, r)
    a = jnp.where(pos == 0, slots[0][0], slots[1][0])
    b = jnp.where(pos == 0, slots[0][1], slots[1][1])
    (q,) = rotations([generator(a, b, True)])
    cut = split(q)
    for p in range(2):
        rows = pl.ds(pl.multiple_of((pos if p == 0 else 1 - pos) * width, width), width)
        high, low = split(dot_split(split(jnp.concatenate([w[a, rows], w[b, rows]], 1)), cut))
        high_ref[p * width:(p + 1) * width] = high
        low_ref[p * width:(p + 1) * width] = low


def apply_kernel(first, count, tile, x_ref, partner_ref, high_ref, low_ref, *rest):
    out_ref, held, sems = rest[-3:]
    rows = x_ref.shape[0]
    blocks = rows // tile
    pos = lax.axis_index("blk")
    copies = []
    for i in range(count):
        there = pl.multiple_of(lax.rem(pos * (blocks // 2) + first + i, blocks) * tile, tile)
        here = slice(i * tile, i * tile + tile)
        data = split(jnp.concatenate([x_ref[pl.ds(there, tile), :], partner_ref[here, :]], 1))
        held[here, :] = dot_split(data, (high_ref[...], low_ref[...]))
        copies.append(
            pltpu.make_async_copy(held.at[here], out_ref.at[pl.ds(there, tile)], sems.at[i])
        )
        copies[-1].start()
    for copy in copies:
        copy.wait()


def apply(first, count, tile, snapshots, partner, high, low, out=None):
    rows, width = snapshots.shape
    extra = () if out is None else (out,)
    return pl.pallas_call(
        functools.partial(apply_kernel, first, count, tile),
        out_shape=jax.ShapeDtypeStruct((rows, width), jnp.float32),
        in_specs=[VMEM] * 4 + [ANY] * len(extra),
        out_specs=ANY,
        scratch_shapes=[
            pltpu.VMEM((count * tile, width), jnp.float32), pltpu.SemaphoreType.DMA((count,)),
        ],
        input_output_aliases={} if out is None else {4: 0},
        compiler_params=pltpu.CompilerParams(vmem_limit_bytes=24 * 1024 * 1024),
        cost_estimate=pl.CostEstimate(
            flops=count * tile * width * width * 48, bytes_accessed=count * tile * width * 16,
            transcendentals=0,
        ),
    )(snapshots, partner, high, low, *extra)


def pair_body(n, snapshots, grades, mover):
    rows, width = snapshots.shape
    share = width // n
    half = rows // 2
    piece = half // CHUNKS
    early = half + EXTRA * piece
    tile = TALL * piece
    f32 = jnp.float32
    dma = pltpu.SemaphoreType.DMA
    whole = pltpu.VMEM((2, n // 2, share, width), f32)
    part = pltpu.VMEM((n // 2, share, width), f32)
    one = pltpu.VMEM((share, width), f32)
    square = jax.ShapeDtypeStruct((width, width), f32)
    squares = jax.ShapeDtypeStruct((2, width, width), f32)
    diag, cross, turn, meta, near, late = pl.pallas_call(
        functools.partial(gram_kernel, n),
        out_shape=(
            squares, square, squares,
            jax.ShapeDtypeStruct((2, 8, width), f32),
            jax.ShapeDtypeStruct((early, width), f32),
            jax.ShapeDtypeStruct((rows - early, width), f32),
        ),
        in_specs=[HBM, HBM, pl.BlockSpec(memory_space=pltpu.SMEM)],
        out_specs=(VMEM, VMEM, VMEM, VMEM, ANY, ANY),
        scratch_shapes=[
            pltpu.VMEM((rows, width), f32), pltpu.VMEM((1, width), jnp.int32),
            pltpu.VMEM((early, width), f32), pltpu.VMEM((8, width), f32), pltpu.VMEM((8, width), f32),
            whole, part, part, part, whole, whole,
            whole, part, part, part, one, one, whole,
            dma((CHUNKS + EXTRA,)), dma((CHUNKS + EXTRA,)),
            dma((2, n // 2)), dma((2, n // 2)), dma((2, n // 2)), dma((2, n // 2)),
            dma((4,)), dma((4,)), dma((3,)), dma((3,)),
            dma((2 * CHUNKS,)), dma((CHUNKS + EXTRA,)), dma((2,)),
        ],
        compiler_params=pltpu.CompilerParams(
            collective_id=0, has_side_effects=True, vmem_limit_bytes=40 * 1024 * 1024
        ),
    )(snapshots, grades.reshape(1, width), mover)
    far = lax.ppermute(late, "blk", [(0, 1), (1, 0)])
    high, low = pl.pallas_call(
        chain_kernel,
        out_shape=(jax.ShapeDtypeStruct((2 * width, width), jnp.bfloat16),) * 2,
        in_specs=[VMEM] * 4,
        out_specs=(VMEM, VMEM),
        scratch_shapes=[
            pltpu.VMEM((16, BW, BW), f32),
            pltpu.VMEM((4, 2 * width, BW), f32),
            pltpu.VMEM((4, BW, BW), f32),
            pltpu.VMEM((4, 8, BW), f32),
        ],
        compiler_params=pltpu.CompilerParams(vmem_limit_bytes=32 * 1024 * 1024),
        cost_estimate=pl.CostEstimate(
            flops=15 * 10**9, bytes_accessed=4 * width * width * 8, transcendentals=0
        ),
    )(diag, cross, turn, meta)
    done = early // tile
    out = apply(0, done, tile, snapshots, near, high, low)
    return apply(done, rows // tile - done, tile, snapshots, far, high, low, out)


def solution(mesh):
    placed = (P("rows", "blk"), P("blk"), P(None, "blk"))
    n = mesh.shape["rows"]
    pairs = mesh.shape["blk"] == 2 and n % 2 == 0 and (2 * BW) % (8 * n) == 0
    body = functools.partial(pair_body, n) if pairs else general_body
    return jax.shard_map(
        body, mesh=mesh, in_specs=placed, out_specs=P("rows", "blk"), check_vma=False
    )
```

```python
import functools

import jax
import jax.numpy as jnp
from jax import lax
from jax.experimental import pallas as pl
from jax.experimental.pallas import tpu as pltpu
from jax.sharding import PartitionSpec as P

BW = 128
ROUNDS = 4
NS_STEPS = 3
CHUNKS = 8
EXTRA = 4
SOON = 1
TALL = 2

epsilon = 1e-06
relaxation = 1.2

MESH = pl.DeviceIdType.MESH
ROWS_DIM = (((0,), (0,)), ((), ()))
PLAIN = (((1,), (0,)), ((), ()))
VMEM = pl.BlockSpec(memory_space=pltpu.VMEM)
ANY = pl.BlockSpec(memory_space=pl.ANY)
HBM = pl.BlockSpec(memory_space=pltpu.HBM)


def from_behind(value, axis, by):
    peers = lax.axis_size(axis)
    return lax.ppermute(value, axis, [(i, (i + by) % peers) for i in range(peers)])


def rotation(cross_gram, squares, labels):
    left_scale = lax.rsqrt(squares[:BW] + epsilon)
    right_scale = lax.rsqrt(squares[BW:] + epsilon)
    grade_gap = jnp.abs(labels[:BW, None] - labels[None, BW:])
    scaled = cross_gram * left_scale[:, None] * right_scale[None, :] / (1.0 + grade_gap)
    magnitude = jnp.sqrt(jnp.sum(scaled * scaled) + epsilon)
    generator = relaxation * scaled / magnitude
    zeros_block = jnp.zeros_like(generator)
    upper_half = jnp.concatenate([zeros_block, generator], 1)
    lower_half = jnp.concatenate([-generator.T, zeros_block], 1)
    iterate = jnp.eye(2 * BW, dtype=generator.dtype) + jnp.concatenate([upper_half, lower_half], 0)
    for sweep in range(NS_STEPS):
        product = lax.dot_general(iterate, iterate, ROWS_DIM, precision=lax.Precision.HIGHEST)
        iterate = 1.5 * iterate - 0.5 * jnp.dot(iterate, product, precision=lax.Precision.HIGHEST)
    return iterate


def statistics(blocks):
    cross_part = lax.dot_general(
        blocks[:, :BW], blocks[:, BW:], ROWS_DIM, precision=lax.Precision.HIGHEST
    )
    square_part = jnp.sum(blocks * blocks, axis=0)
    return lax.psum((cross_part, square_part), "rows")


def assemble(first, incoming, staying):
    return jnp.where(
        first, jnp.concatenate([incoming, staying], -1), jnp.concatenate([staying, incoming], -1)
    )


def general_body(snapshots, grades, mover):
    blocks = snapshots
    labels = grades.astype(jnp.float32)
    for round_index in range(ROUNDS):
        cross_gram, squares = statistics(blocks)
        rotator = rotation(cross_gram, squares, labels)
        blocks = jnp.dot(blocks, rotator, precision=lax.Precision.HIGHEST)
        if round_index + 1 < ROUNDS:
            first = mover[round_index, 0] == 0
            move_label = jnp.where(first, labels[:BW], labels[BW:])
            stay_label = jnp.where(first, labels[BW:], labels[:BW])
            moving = jnp.where(first, blocks[:, :BW], blocks[:, BW:])
            staying = jnp.where(first, blocks[:, BW:], blocks[:, :BW])
            incoming, came_label = from_behind((moving, move_label), "blk", 1)
            blocks = assemble(first, incoming, staying)
            labels = assemble(first, came_label, stay_label)
    return blocks


def split(value):
    high = value.astype(jnp.bfloat16)
    return high, (value - high.astype(jnp.float32)).astype(jnp.bfloat16)


def dot_split(a, b, dims=PLAIN):
    (ah, al), (bh, bl) = a, b
    mul = functools.partial(lax.dot_general, dimension_numbers=dims, preferred_element_type=jnp.float32)
    return mul(ah, bh) + (mul(ah, bl) + mul(al, bh))


def dot3(a, b, dims=PLAIN):
    return dot_split(split(a), split(b), dims)


def dot6(a, b, dims=PLAIN):
    return lax.dot_general(
        a, b, dims, precision=lax.Precision.HIGHEST, preferred_element_type=jnp.float32
    )


def gram_kernel(
    n, x_hbm, grade_ref, mover_ref, diag_ref, cross_ref, turn_ref, meta_out, near_ref, late_ref,
    x_ref, grade, came, meta, meta_got, dpart, dgot, dmid, dnear, dfull, dother,
    cpart, cgot, cmid, cnear, cmine, cother, cfull,
    x_send, x_recv, rs_send, rs_recv, ag_send, ag_recv, sib_send, sib_recv, one_send, one_recv,
    load_sem, near_sem, side_sem,
):
    pos, me = lax.axis_index("blk"), lax.axis_index("rows")
    other = 1 - pos
    core, group = lax.rem(me, 2), me // 2
    groups = n // 2
    rows, width = x_ref.shape
    half = rows // 2
    piece = half // CHUNKS
    share = width // n
    partner, sibling = (other, me), (pos, me + 1 - 2 * core)
    peers = [None] + [lax.rem(group + k, groups) for k in range(1, groups)]

    grade_load = pltpu.make_async_copy(grade_ref, grade, side_sem.at[0])
    grade_load.start()
    loads = []
    for t in range(rows // piece):
        at = pl.ds(t * piece, piece)
        loads.append(pltpu.make_async_copy(x_hbm.at[at], x_ref.at[at], load_sem.at[t]))
        loads[-1].start()

    barrier = pltpu.get_barrier_semaphore()
    for peer in peers[1:]:
        pl.semaphore_signal(barrier, inc=1, device_id=(pos, 2 * peer + core), device_id_type=MESH)
    for device in (partner, sibling):
        pl.semaphore_signal(barrier, inc=1, device_id=device, device_id_type=MESH)
    meta[...] = jnp.zeros_like(meta)
    grade_load.wait()
    meta[0:1, :] = grade[...].astype(jnp.float32)
    for r in range(ROUNDS - 1):
        meta[r + 1:r + 2, :] = jnp.full((1, width), mover_ref[r, 0], jnp.int32).astype(jnp.float32)
    pl.semaphore_wait(barrier, groups + 1)

    def remote(src, dst, send, recv, device):
        copy = pltpu.make_async_remote_copy(
            src_ref=src, dst_ref=dst, send_sem=send, recv_sem=recv,
            device_id=device, device_id_type=MESH,
        )
        copy.start()
        return copy

    def swap(c):
        start = lax.rem(other * half + c * piece, rows)
        source = x_hbm.at[pl.ds(pl.multiple_of(start, piece), piece)]
        return remote(source, came.at[pl.ds(c * piece, piece)], x_send.at[c], x_recv.at[c], partner)

    labels = remote(meta, meta_got, one_send.at[0], one_recv.at[0], partner)
    swaps = [swap(c) for c in range(CHUNKS)]

    def pair_up(part, got, which):
        return remote(part.at[1 - core], got, sib_send.at[which], sib_recv.at[which], sibling)

    def scatter(mid, near, which):
        return [
            remote(
                mid.at[peers[k]], near.at[k], rs_send.at[which, k], rs_recv.at[which, k],
                (pos, 2 * peers[k] + core),
            )
            for k in range(1, groups)
        ]

    def summed(mid, near, copies):
        total = mid[group]
        for k in range(1, groups):
            copies[k - 1].wait()
            total = total + near[k]
        return total

    def gather(full, which):
        return [
            remote(
                full.at[core, group], full.at[core, group], ag_send.at[which, k],
                ag_recv.at[which, k], (pos, 2 * peers[k] + core),
            )
            for k in range(1, groups)
        ]

    def hand_over(full, copies, which):
        for copy in copies:
            copy.wait()
        return remote(full.at[core], full.at[core], sib_send.at[which], sib_recv.at[which], sibling)

    kept = []

    def keep(c):
        at = pl.ds(c * piece, piece)
        kept.append(pltpu.make_async_copy(came.at[at], near_ref.at[at], near_sem.at[c]))
        kept[-1].start()

    def cross(c, count=2):
        for i in range(c, c + count):
            swaps[i].wait()
            keep(i)
        mine = x_ref[pl.ds(pl.multiple_of(pos * half + c * piece, piece), count * piece), :]
        theirs = came[c * piece:(c + count) * piece, :]
        left = jnp.where(pos == 0, mine, theirs)
        right = jnp.where(pos == 0, theirs, mine)
        return dot3(left.T, right)

    mul = functools.partial(lax.dot_general, dimension_numbers=PLAIN, preferred_element_type=jnp.float32)
    own = jnp.zeros((width, width), jnp.float32)
    rest = jnp.zeros((width, width), jnp.float32)
    tall = half // 2
    for t in range(rows // tall):
        for i in range(t * (tall // piece), (t + 1) * (tall // piece)):
            loads[i].wait()
        block = x_ref[t * tall:(t + 1) * tall, :]
        high, low = split(block)
        across = block.T.astype(jnp.bfloat16)
        own = own + mul(across, high)
        rest = rest + mul(across, low)
    own = own + rest + rest.T
    dpart[...] = own.reshape(2, groups, share, width)
    copy = pair_up(dpart, dgot, 0)
    begin = pl.multiple_of(pos * half + EXTRA * piece, piece)
    aside = pltpu.make_async_copy(
        x_ref.at[pl.ds(begin, half - EXTRA * piece)], late_ref, side_sem.at[1]
    )
    aside.start()
    total = cross(0)
    copy.wait()
    dmid[...] = dpart[core] + dgot[...]
    copies = scatter(dmid, dnear, 0)
    total = total + cross(2)
    dfull[core, group] = summed(dmid, dnear, copies)
    copies = gather(dfull, 0)
    total = total + cross(4)
    copy = hand_over(dfull, copies, 1)
    copy.wait()
    d_swap = remote(dfull, dother, one_send.at[1], one_recv.at[1], partner)
    late = [swap(c) for c in range(CHUNKS, CHUNKS + SOON)]
    for c in range(6, CHUNKS, 2):
        total = total + cross(c)
    cpart[...] = total.reshape(2, groups, share, width)
    copy = pair_up(cpart, cgot, 2)
    diag_ref[pos] = dfull[...].reshape(width, width)
    labels.wait()
    meta_out[pos] = meta[...]
    meta_out[other] = meta_got[...]
    copy.wait()
    cmid[...] = cpart[core] + cgot[...]
    copies = scatter(cmid, cnear, 1)
    unit = eye(BW)

    def begin_round(p):
        diag = diag_ref[p]
        left_square = jnp.sum(diag[:BW, :BW] * unit, axis=1, keepdims=True)
        right_square = jnp.sum(diag[BW:, BW:] * unit, axis=0, keepdims=True)
        left_label = jnp.broadcast_to(meta_out[p, 0:1, :BW], (BW, BW)).T
        (q,) = rotations(
            [polar(diag[:BW, BW:], left_square, right_square, left_label, meta_out[p, 0:1, BW:])]
        )
        turn_ref[p] = q
        diag_ref[p] = dot6(q.T, dot6(diag, q))

    begin_round(pos)
    cmine[...] = summed(cmid, cnear, copies)
    c_swap = remote(cmine, cother, one_send.at[2], one_recv.at[2], partner)
    late += [swap(c) for c in range(CHUNKS + SOON, CHUNKS + EXTRA)]
    d_swap.wait()
    diag_ref[other] = dother[...].reshape(width, width)
    c_swap.wait()
    cfull[core, group] = cmine[...] + cother[...]
    copies = gather(cfull, 1)
    begin_round(other)
    copy = hand_over(cfull, copies, 3)
    for c in range(EXTRA):
        late[c].wait()
        keep(CHUNKS + c)
    copy.wait()
    cross_ref[...] = cfull[...].reshape(width, width)
    aside.wait()
    for copy in kept:
        copy.wait()


def polar(cross_gram, left_square, right_square, left_label, right_label):
    left_scale = lax.rsqrt(left_square + epsilon)
    right_scale = lax.rsqrt(right_square + epsilon)
    scaled = cross_gram * left_scale * right_scale / (1.0 + jnp.abs(left_label - right_label))
    magnitude = jnp.sqrt(jnp.sum(scaled * scaled, keepdims=True) + epsilon)
    return relaxation * scaled / magnitude


def eye(n):
    return (
        lax.broadcasted_iota(jnp.int32, (n, n), 0) == lax.broadcasted_iota(jnp.int32, (n, n), 1)
    ).astype(jnp.float32)


def rotations(generators):
    unit = eye(BW)
    signs = [split(b) for b in generators]
    turned = [split(b.T) for b in generators]
    norm = []
    for b, bt in zip(signs, turned):
        norm.append(unit + dot_split(b, bt))
        norm.append(unit + dot_split(bt, b))
    gain = None
    for sweep in range(NS_STEPS):
        factor = [1.5 * unit - 0.5 * v for v in norm]
        cut = [split(f) for f in factor]
        last = sweep + 1 == NS_STEPS
        if last:
            edge = [dot_split(cut[2 * i], split(e)) for i, e in enumerate(edge)]
        else:
            parts = [split(v) for v in norm]
            inner = [2.25 * unit - 1.5 * v + 0.25 * dot_split(p, p) for v, p in zip(norm, parts)]
            norm = [dot_split(p, split(v)) for p, v in zip(parts, inner)]
        if gain is None:
            gain = factor
        else:
            gain = [dot_split(split(g), f) for g, f in zip(gain, cut)]
        if sweep + 2 == NS_STEPS:
            edge = [dot_split(split(gain[2 * i]), b) for i, b in enumerate(signs)]
    out = []
    for i, e in enumerate(edge):
        upper = jnp.concatenate([gain[2 * i], e], 1)
        lower = jnp.concatenate([-e.T, gain[2 * i + 1]], 1)
        out.append(jnp.concatenate([upper, lower], 0))
    return out


def place(first, i, tile, rows):
    blocks = rows // tile
    at = lax.rem(lax.axis_index("blk") * (blocks // 2) + first + i, blocks)
    return pl.ds(pl.multiple_of(at * tile, tile), tile)


def fetch(first, count, tile, x_hbm, x_ref, sems):
    loads = []
    for i in range(count):
        source = x_hbm.at[place(first, i, tile, x_hbm.shape[0])]
        loads.append(pltpu.make_async_copy(source, x_ref.at[pl.ds(i * tile, tile)], sems.at[i]))
        loads[-1].start()
    return loads


def turn_rows(
    first, count, tile, loads, x_ref, partner_ref, high_ref, low_ref, held, out_ref, sems
):
    copies = []
    for i in range(count):
        here = slice(i * tile, i * tile + tile)
        loads[i].wait()
        data = split(jnp.concatenate([x_ref[here, :], partner_ref[here, :]], 1))
        held[here, :] = dot_split(data, (high_ref[...], low_ref[...]))
        target = out_ref.at[place(first, i, tile, out_ref.shape[0])]
        copies.append(pltpu.make_async_copy(held.at[pl.ds(i * tile, tile)], target, sems.at[i]))
        copies[-1].start()
    for copy in copies:
        copy.wait()


def chain_kernel(
    count, tile, diag_ref, cross_ref, turn_ref, meta_ref, x_hbm, near_ref, out_ref, high_ref, low_ref,
    g, w, lab, squares, x_ref, held, load_sem, store_sem,
):
    pos = lax.axis_index("blk")
    loads = fetch(0, count, tile, x_hbm, x_ref, load_sem)
    width = 2 * BW
    small = eye(BW)
    between = dot6(turn_ref[0].T, dot6(cross_ref[...], turn_ref[1]))
    for i in range(4):
        p, s = divmod(i, 2)
        rows = slice(s * BW, s * BW + BW)
        for j in range(4):
            q, t = divmod(j, 2)
            cols = slice(t * BW, t * BW + BW)
            if p == q:
                g[4 * i + j] = diag_ref[p, rows, cols]
            elif p == 0:
                g[4 * i + j] = between[rows, cols]
                g[4 * j + i] = between[rows, cols].T
        lab[i] = jnp.broadcast_to(meta_ref[p, 0:1, rows], (BW, BW))
        w[i] = jnp.zeros((2 * width, BW), jnp.float32)
        w[i, p * width:(p + 1) * width] = turn_ref[p, :, rows]

    def generator(a, b, known=False):
        if known:
            left_square = jnp.broadcast_to(squares[a, 0:1], (BW, BW)).T
            right_square = squares[b, 0:1]
        else:
            left_square = jnp.sum(g[4 * a + a] * small, axis=1, keepdims=True)
            right_square = jnp.sum(g[4 * b + b] * small, axis=0, keepdims=True)
        return polar(g[4 * a + b], left_square, right_square, lab[a].T, lab[b])

    def step(slots, r):
        first = [jnp.max(meta_ref[p, r + 1:r + 2, :BW]) < 0.5 for p in range(2)]
        moving = [jnp.where(first[p], slots[p][0], slots[p][1]) for p in range(2)]
        staying = [jnp.where(first[p], slots[p][1], slots[p][0]) for p in range(2)]
        return [
            [
                jnp.where(first[p], moving[1 - p], staying[p]),
                jnp.where(first[p], staying[p], moving[1 - p]),
            ]
            for p in range(2)
        ]

    slots = step([[0, 1], [2, 3]], 0)
    for r in range(1, ROUNDS - 1):
        qs = rotations([generator(*slots[p]) for p in range(2)])
        backs = [q.T for q in qs]
        last = r + 2 == ROUNDS
        for p, q in ((0, 0), (1, 1), (0, 1)):
            (a, b), (c, d) = slots[p], slots[q]
            upper = jnp.concatenate([g[4 * a + c], g[4 * a + d]], 1)
            lower = jnp.concatenate([g[4 * b + c], g[4 * b + d]], 1)
            block = jnp.concatenate([upper, lower], 0)
            block = dot6(block, qs[q])
            if last and p == q:
                square = jnp.sum(qs[p] * block, axis=0, keepdims=True)
                squares[a] = jnp.broadcast_to(square[:, :BW], (8, BW))
                squares[b] = jnp.broadcast_to(square[:, BW:], (8, BW))
                continue
            block = dot6(backs[p], block)
            for i, e in enumerate((a, b)):
                for j, f in enumerate((c, d)):
                    value = block[i * BW:(i + 1) * BW, j * BW:(j + 1) * BW]
                    g[4 * e + f] = value
                    if p != q:
                        g[4 * f + e] = value.T
        for p in range(2):
            a, b = slots[p]
            both = dot3(jnp.concatenate([w[a], w[b]], 1), qs[p])
            w[a] = both[:, :BW]
            w[b] = both[:, BW:]
        slots = step(slots, r)
    a = jnp.where(pos == 0, slots[0][0], slots[1][0])
    b = jnp.where(pos == 0, slots[0][1], slots[1][1])
    (q,) = rotations([generator(a, b, True)])
    cut = split(q)
    for p in range(2):
        rows = pl.ds(pl.multiple_of((pos if p == 0 else 1 - pos) * width, width), width)
        high, low = split(dot_split(split(jnp.concatenate([w[a, rows], w[b, rows]], 1)), cut))
        high_ref[p * width:(p + 1) * width] = high
        low_ref[p * width:(p + 1) * width] = low
    turn_rows(0, count, tile, loads, x_ref, near_ref, high_ref, low_ref, held, out_ref, store_sem)


def apply_kernel(
    first, count, tile, x_hbm, partner_ref, high_ref, low_ref, into_ref, out_ref,
    x_ref, held, load_sem, store_sem,
):
    loads = fetch(first, count, tile, x_hbm, x_ref, load_sem)
    turn_rows(
        first, count, tile, loads, x_ref, partner_ref, high_ref, low_ref, held, out_ref, store_sem
    )


def pair_body(n, snapshots, grades, mover):
    rows, width = snapshots.shape
    share = width // n
    half = rows // 2
    piece = half // CHUNKS
    early = half + EXTRA * piece
    tile = TALL * piece
    f32 = jnp.float32
    dma = pltpu.SemaphoreType.DMA
    whole = pltpu.VMEM((2, n // 2, share, width), f32)
    part = pltpu.VMEM((n // 2, share, width), f32)
    one = pltpu.VMEM((share, width), f32)
    square = jax.ShapeDtypeStruct((width, width), f32)
    squares = jax.ShapeDtypeStruct((2, width, width), f32)
    diag, cross, turn, meta, near, late = pl.pallas_call(
        functools.partial(gram_kernel, n),
        out_shape=(
            squares, square, squares,
            jax.ShapeDtypeStruct((2, 8, width), f32),
            jax.ShapeDtypeStruct((early, width), f32),
            jax.ShapeDtypeStruct((rows - early, width), f32),
        ),
        in_specs=[HBM, HBM, pl.BlockSpec(memory_space=pltpu.SMEM)],
        out_specs=(VMEM, VMEM, VMEM, VMEM, ANY, ANY),
        scratch_shapes=[
            pltpu.VMEM((rows, width), f32), pltpu.VMEM((1, width), jnp.int32),
            pltpu.VMEM((early, width), f32), pltpu.VMEM((8, width), f32), pltpu.VMEM((8, width), f32),
            whole, part, part, part, whole, whole,
            whole, part, part, part, one, one, whole,
            dma((CHUNKS + EXTRA,)), dma((CHUNKS + EXTRA,)),
            dma((2, n // 2)), dma((2, n // 2)), dma((2, n // 2)), dma((2, n // 2)),
            dma((4,)), dma((4,)), dma((3,)), dma((3,)),
            dma((2 * CHUNKS,)), dma((CHUNKS + EXTRA,)), dma((2,)),
        ],
        compiler_params=pltpu.CompilerParams(
            collective_id=0, has_side_effects=True, vmem_limit_bytes=40 * 1024 * 1024
        ),
    )(snapshots, grades.reshape(1, width), mover)
    far = lax.ppermute(late, "blk", [(0, 1), (1, 0)])
    done = early // tile
    left = rows // tile - done
    basis = jax.ShapeDtypeStruct((rows, width), f32)
    weights = jax.ShapeDtypeStruct((2 * width, width), jnp.bfloat16)

    def room(count):
        return [
            pltpu.VMEM((count * tile, width), f32), pltpu.VMEM((count * tile, width), f32),
            dma((count,)), dma((count,)),
        ]

    out, high, low = pl.pallas_call(
        functools.partial(chain_kernel, done, tile),
        out_shape=(basis, weights, weights),
        in_specs=[VMEM] * 4 + [HBM, VMEM],
        out_specs=(HBM, VMEM, VMEM),
        scratch_shapes=[
            pltpu.VMEM((16, BW, BW), f32),
            pltpu.VMEM((4, 2 * width, BW), f32),
            pltpu.VMEM((4, BW, BW), f32),
            pltpu.VMEM((4, 8, BW), f32),
        ] + room(done),
        compiler_params=pltpu.CompilerParams(vmem_limit_bytes=36 * 1024 * 1024),
        cost_estimate=pl.CostEstimate(
            flops=18 * 10**9, bytes_accessed=4 * width * width * 8, transcendentals=0
        ),
    )(diag, cross, turn, meta, snapshots, near)
    return pl.pallas_call(
        functools.partial(apply_kernel, done, left, tile),
        out_shape=basis,
        in_specs=[HBM, VMEM, VMEM, VMEM, HBM],
        out_specs=HBM,
        scratch_shapes=room(left),
        input_output_aliases={4: 0},
        compiler_params=pltpu.CompilerParams(vmem_limit_bytes=24 * 1024 * 1024),
    )(snapshots, far, high, low, out)


def solution(mesh):
    placed = (P("rows", "blk"), P("blk"), P(None, "blk"))
    n = mesh.shape["rows"]
    pairs = mesh.shape["blk"] == 2 and n % 2 == 0 and (2 * BW) % (8 * n) == 0
    body = functools.partial(pair_body, n) if pairs else general_body
    return jax.shard_map(
        body, mesh=mesh, in_specs=placed, out_specs=P("rows", "blk"), check_vma=False
    )
```

```python
import functools

import jax
import jax.numpy as jnp
from jax import lax
from jax.experimental import pallas as pl
from jax.experimental.pallas import tpu as pltpu
from jax.sharding import PartitionSpec as P

BW = 128
ROUNDS = 4
NS_STEPS = 3
CHUNKS = 8
EXTRA = 4
SOON = 1
TALL = 2

epsilon = 1e-06
relaxation = 1.2

MESH = pl.DeviceIdType.MESH
ROWS_DIM = (((0,), (0,)), ((), ()))
PLAIN = (((1,), (0,)), ((), ()))
VMEM = pl.BlockSpec(memory_space=pltpu.VMEM)
ANY = pl.BlockSpec(memory_space=pl.ANY)
HBM = pl.BlockSpec(memory_space=pltpu.HBM)


def from_behind(value, axis, by):
    peers = lax.axis_size(axis)
    return lax.ppermute(value, axis, [(i, (i + by) % peers) for i in range(peers)])


def rotation(cross_gram, squares, labels):
    left_scale = lax.rsqrt(squares[:BW] + epsilon)
    right_scale = lax.rsqrt(squares[BW:] + epsilon)
    grade_gap = jnp.abs(labels[:BW, None] - labels[None, BW:])
    scaled = cross_gram * left_scale[:, None] * right_scale[None, :] / (1.0 + grade_gap)
    magnitude = jnp.sqrt(jnp.sum(scaled * scaled) + epsilon)
    generator = relaxation * scaled / magnitude
    zeros_block = jnp.zeros_like(generator)
    upper_half = jnp.concatenate([zeros_block, generator], 1)
    lower_half = jnp.concatenate([-generator.T, zeros_block], 1)
    iterate = jnp.eye(2 * BW, dtype=generator.dtype) + jnp.concatenate([upper_half, lower_half], 0)
    for sweep in range(NS_STEPS):
        product = lax.dot_general(iterate, iterate, ROWS_DIM, precision=lax.Precision.HIGHEST)
        iterate = 1.5 * iterate - 0.5 * jnp.dot(iterate, product, precision=lax.Precision.HIGHEST)
    return iterate


def statistics(blocks):
    cross_part = lax.dot_general(
        blocks[:, :BW], blocks[:, BW:], ROWS_DIM, precision=lax.Precision.HIGHEST
    )
    square_part = jnp.sum(blocks * blocks, axis=0)
    return lax.psum((cross_part, square_part), "rows")


def assemble(first, incoming, staying):
    return jnp.where(
        first, jnp.concatenate([incoming, staying], -1), jnp.concatenate([staying, incoming], -1)
    )


def general_body(snapshots, grades, mover):
    blocks = snapshots
    labels = grades.astype(jnp.float32)
    for round_index in range(ROUNDS):
        cross_gram, squares = statistics(blocks)
        rotator = rotation(cross_gram, squares, labels)
        blocks = jnp.dot(blocks, rotator, precision=lax.Precision.HIGHEST)
        if round_index + 1 < ROUNDS:
            first = mover[round_index, 0] == 0
            move_label = jnp.where(first, labels[:BW], labels[BW:])
            stay_label = jnp.where(first, labels[BW:], labels[:BW])
            moving = jnp.where(first, blocks[:, :BW], blocks[:, BW:])
            staying = jnp.where(first, blocks[:, BW:], blocks[:, :BW])
            incoming, came_label = from_behind((moving, move_label), "blk", 1)
            blocks = assemble(first, incoming, staying)
            labels = assemble(first, came_label, stay_label)
    return blocks


def split(value):
    high = value.astype(jnp.bfloat16)
    return high, (value - high.astype(jnp.float32)).astype(jnp.bfloat16)


def dot_split(a, b, dims=PLAIN):
    (ah, al), (bh, bl) = a, b
    mul = functools.partial(lax.dot_general, dimension_numbers=dims, preferred_element_type=jnp.float32)
    return mul(ah, bh) + (mul(ah, bl) + mul(al, bh))


def dot3(a, b, dims=PLAIN):
    return dot_split(split(a), split(b), dims)


def dot6(a, b, dims=PLAIN):
    return lax.dot_general(
        a, b, dims, precision=lax.Precision.HIGHEST, preferred_element_type=jnp.float32
    )


def gram_kernel(
    n, x_ref, grade_ref, mover_ref, diag_ref, cross_ref, turn_ref, meta_out, near_ref, late_ref,
    meta, meta_got, dpart, dgot, dmid, dnear, dfull, dother,
    cpart, cgot, cmid, cnear, cmine, cother, cfull,
    x_send, x_recv, rs_send, rs_recv, ag_send, ag_recv, sib_send, sib_recv, one_send, one_recv,
    side_sem,
):
    pos, me = lax.axis_index("blk"), lax.axis_index("rows")
    other = 1 - pos
    core, group = lax.rem(me, 2), me // 2
    groups = n // 2
    rows, width = x_ref.shape
    half = rows // 2
    piece = half // CHUNKS
    share = width // n
    partner, sibling = (other, me), (pos, me + 1 - 2 * core)
    peers = [None] + [lax.rem(group + k, groups) for k in range(1, groups)]

    barrier = pltpu.get_barrier_semaphore()
    for peer in peers[1:]:
        pl.semaphore_signal(barrier, inc=1, device_id=(pos, 2 * peer + core), device_id_type=MESH)
    for device in (partner, sibling):
        pl.semaphore_signal(barrier, inc=1, device_id=device, device_id_type=MESH)
    meta[...] = jnp.zeros_like(meta)
    meta[0:1, :] = grade_ref[...].astype(jnp.float32)
    for r in range(ROUNDS - 1):
        meta[r + 1:r + 2, :] = jnp.full((1, width), mover_ref[r, 0], jnp.int32).astype(jnp.float32)
    pl.semaphore_wait(barrier, groups + 1)

    def remote(src, dst, send, recv, device):
        copy = pltpu.make_async_remote_copy(
            src_ref=src, dst_ref=dst, send_sem=send, recv_sem=recv,
            device_id=device, device_id_type=MESH,
        )
        copy.start()
        return copy

    def swap(c):
        start = lax.rem(other * half + c * piece, rows)
        source = x_ref.at[pl.ds(pl.multiple_of(start, piece), piece)]
        return remote(source, near_ref.at[pl.ds(c * piece, piece)], x_send.at[c], x_recv.at[c], partner)

    labels = remote(meta, meta_got, one_send.at[0], one_recv.at[0], partner)
    swaps = [swap(c) for c in range(CHUNKS)]

    def pair_up(part, got, which):
        return remote(part.at[1 - core], got, sib_send.at[which], sib_recv.at[which], sibling)

    def scatter(mid, near, which):
        return [
            remote(
                mid.at[peers[k]], near.at[k], rs_send.at[which, k], rs_recv.at[which, k],
                (pos, 2 * peers[k] + core),
            )
            for k in range(1, groups)
        ]

    def summed(mid, near, copies):
        total = mid[group]
        for k in range(1, groups):
            copies[k - 1].wait()
            total = total + near[k]
        return total

    def gather(full, which):
        return [
            remote(
                full.at[core, group], full.at[core, group], ag_send.at[which, k],
                ag_recv.at[which, k], (pos, 2 * peers[k] + core),
            )
            for k in range(1, groups)
        ]

    def hand_over(full, copies, which):
        for copy in copies:
            copy.wait()
        return remote(full.at[core], full.at[core], sib_send.at[which], sib_recv.at[which], sibling)

    def cross(c):
        swaps[c].wait()
        mine = x_ref[pl.ds(pl.multiple_of(pos * half + c * piece, piece), piece), :]
        theirs = near_ref[c * piece:(c + 1) * piece, :]
        left = jnp.where(pos == 0, mine, theirs)
        right = jnp.where(pos == 0, theirs, mine)
        return dot3(left, right, ROWS_DIM)

    own = jnp.zeros((width, width), jnp.float32)
    for t in range(rows // piece):
        block = split(x_ref[t * piece:(t + 1) * piece, :])
        own = own + dot_split(block, block, ROWS_DIM)
    dpart[...] = own.reshape(2, groups, share, width)
    copy = pair_up(dpart, dgot, 0)
    total = cross(0) + cross(1)
    copy.wait()
    dmid[...] = dpart[core] + dgot[...]
    copies = scatter(dmid, dnear, 0)
    total = total + cross(2)
    dfull[core, group] = summed(dmid, dnear, copies)
    copies = gather(dfull, 0)
    total = total + cross(3) + cross(4)
    copy = hand_over(dfull, copies, 1)
    copy.wait()
    d_swap = remote(dfull, dother, one_send.at[1], one_recv.at[1], partner)
    late = [swap(c) for c in range(CHUNKS, CHUNKS + SOON)]
    for c in range(5, CHUNKS):
        total = total + cross(c)
    cpart[...] = total.reshape(2, groups, share, width)
    copy = pair_up(cpart, cgot, 2)
    diag_ref[pos] = dfull[...].reshape(width, width)
    labels.wait()
    meta_out[pos] = meta[...]
    meta_out[other] = meta_got[...]
    copy.wait()
    cmid[...] = cpart[core] + cgot[...]
    copies = scatter(cmid, cnear, 1)
    begin = pl.multiple_of(pos * half + EXTRA * piece, piece)
    aside = pltpu.make_async_copy(
        x_ref.at[pl.ds(begin, half - EXTRA * piece)], late_ref, side_sem.at[1]
    )
    aside.start()
    unit = eye(BW)

    def begin_round(p):
        diag = diag_ref[p]
        left_square = jnp.sum(diag[:BW, :BW] * unit, axis=1, keepdims=True)
        right_square = jnp.sum(diag[BW:, BW:] * unit, axis=0, keepdims=True)
        left_label = jnp.broadcast_to(meta_out[p, 0:1, :BW], (BW, BW)).T
        (q,) = rotations(
            [polar(diag[:BW, BW:], left_square, right_square, left_label, meta_out[p, 0:1, BW:])]
        )
        turn_ref[p] = q
        diag_ref[p] = dot6(q, dot6(diag, q), ROWS_DIM)

    begin_round(pos)
    cmine[...] = summed(cmid, cnear, copies)
    c_swap = remote(cmine, cother, one_send.at[2], one_recv.at[2], partner)
    late += [swap(c) for c in range(CHUNKS + SOON, CHUNKS + EXTRA)]
    d_swap.wait()
    diag_ref[other] = dother[...].reshape(width, width)
    c_swap.wait()
    cfull[core, group] = cmine[...] + cother[...]
    copies = gather(cfull, 1)
    begin_round(other)
    copy = hand_over(cfull, copies, 3)
    for c in range(EXTRA):
        late[c].wait()
    copy.wait()
    cross_ref[...] = cfull[...].reshape(width, width)
    aside.wait()


def polar(cross_gram, left_square, right_square, left_label, right_label):
    left_scale = lax.rsqrt(left_square + epsilon)
    right_scale = lax.rsqrt(right_square + epsilon)
    scaled = cross_gram * left_scale * right_scale / (1.0 + jnp.abs(left_label - right_label))
    magnitude = jnp.sqrt(jnp.sum(scaled * scaled, keepdims=True) + epsilon)
    return relaxation * scaled / magnitude


def eye(n):
    return (
        lax.broadcasted_iota(jnp.int32, (n, n), 0) == lax.broadcasted_iota(jnp.int32, (n, n), 1)
    ).astype(jnp.float32)


def rotations(generators):
    unit = eye(BW)
    signs = [split(b) for b in generators]
    turned = [split(b.T) for b in generators]
    norm = []
    for b, bt in zip(signs, turned):
        norm.append(unit + dot_split(b, bt))
        norm.append(unit + dot_split(bt, b))
    gain = None
    for sweep in range(NS_STEPS):
        factor = [1.5 * unit - 0.5 * v for v in norm]
        cut = [split(f) for f in factor]
        last = sweep + 1 == NS_STEPS
        if last:
            edge = [dot_split(cut[2 * i], split(e)) for i, e in enumerate(edge)]
        else:
            parts = [split(v) for v in norm]
            inner = [2.25 * unit - 1.5 * v + 0.25 * dot_split(p, p) for v, p in zip(norm, parts)]
            norm = [dot_split(p, split(v)) for p, v in zip(parts, inner)]
        if gain is None:
            gain = factor
        else:
            gain = [dot_split(split(g), f) for g, f in zip(gain, cut)]
        if sweep + 2 == NS_STEPS:
            edge = [dot_split(split(gain[2 * i]), b) for i, b in enumerate(signs)]
    out = []
    for i, e in enumerate(edge):
        upper = jnp.concatenate([gain[2 * i], e], 1)
        lower = jnp.concatenate([-e.T, gain[2 * i + 1]], 1)
        out.append(jnp.concatenate([upper, lower], 0))
    return out


def chain_kernel(diag_ref, cross_ref, turn_ref, meta_ref, high_ref, low_ref, g, w, lab, squares):
    pos = lax.axis_index("blk")
    width = 2 * BW
    small = eye(BW)
    between = dot6(turn_ref[0], dot6(cross_ref[...], turn_ref[1]), ROWS_DIM)
    for i in range(4):
        p, s = divmod(i, 2)
        rows = slice(s * BW, s * BW + BW)
        for j in range(4):
            q, t = divmod(j, 2)
            cols = slice(t * BW, t * BW + BW)
            if p == q:
                g[4 * i + j] = diag_ref[p, rows, cols]
            elif p == 0:
                g[4 * i + j] = between[rows, cols]
                g[4 * j + i] = between[rows, cols].T
        lab[i] = jnp.broadcast_to(meta_ref[p, 0:1, rows], (BW, BW))
        w[i] = jnp.zeros((2 * width, BW), jnp.float32)
        w[i, p * width:(p + 1) * width] = turn_ref[p, :, rows]

    def generator(a, b, known=False):
        if known:
            left_square = jnp.broadcast_to(squares[a, 0:1], (BW, BW)).T
            right_square = squares[b, 0:1]
        else:
            left_square = jnp.sum(g[4 * a + a] * small, axis=1, keepdims=True)
            right_square = jnp.sum(g[4 * b + b] * small, axis=0, keepdims=True)
        return polar(g[4 * a + b], left_square, right_square, lab[a].T, lab[b])

    def step(slots, r):
        first = [jnp.max(meta_ref[p, r + 1:r + 2, :BW]) < 0.5 for p in range(2)]
        moving = [jnp.where(first[p], slots[p][0], slots[p][1]) for p in range(2)]
        staying = [jnp.where(first[p], slots[p][1], slots[p][0]) for p in range(2)]
        return [
            [
                jnp.where(first[p], moving[1 - p], staying[p]),
                jnp.where(first[p], staying[p], moving[1 - p]),
            ]
            for p in range(2)
        ]

    slots = step([[0, 1], [2, 3]], 0)
    for r in range(1, ROUNDS - 1):
        qs = rotations([generator(*slots[p]) for p in range(2)])
        last = r + 2 == ROUNDS
        for p, q in ((0, 0), (1, 1), (0, 1)):
            (a, b), (c, d) = slots[p], slots[q]
            upper = jnp.concatenate([g[4 * a + c], g[4 * a + d]], 1)
            lower = jnp.concatenate([g[4 * b + c], g[4 * b + d]], 1)
            block = jnp.concatenate([upper, lower], 0)
            block = dot6(block, qs[q])
            if last and p == q:
                square = jnp.sum(qs[p] * block, axis=0, keepdims=True)
                squares[a] = jnp.broadcast_to(square[:, :BW], (8, BW))
                squares[b] = jnp.broadcast_to(square[:, BW:], (8, BW))
                continue
            block = dot6(qs[p], block, ROWS_DIM)
            for i, e in enumerate((a, b)):
                for j, f in enumerate((c, d)):
                    value = block[i * BW:(i + 1) * BW, j * BW:(j + 1) * BW]
                    g[4 * e + f] = value
                    if p != q:
                        g[4 * f + e] = value.T
        for p in range(2):
            a, b = slots[p]
            both = dot3(jnp.concatenate([w[a], w[b]], 1), qs[p])
            w[a] = both[:, :BW]
            w[b] = both[:, BW:]
        slots = step(slots, r)
    a = jnp.where(pos == 0, slots[0][0], slots[1][0])
    b = jnp.where(pos == 0, slots[0][1], slots[1][1])
    (q,) = rotations([generator(a, b, True)])
    cut = split(q)
    for p in range(2):
        rows = pl.ds(pl.multiple_of((pos if p == 0 else 1 - pos) * width, width), width)
        high, low = split(dot_split(split(jnp.concatenate([w[a, rows], w[b, rows]], 1)), cut))
        high_ref[p * width:(p + 1) * width] = high
        low_ref[p * width:(p + 1) * width] = low


def apply_kernel(first, count, tile, x_ref, partner_ref, high_ref, low_ref, *rest):
    out_ref, held, sems = rest[-3:]
    rows = x_ref.shape[0]
    blocks = rows // tile
    pos = lax.axis_index("blk")
    copies = []
    for i in range(count):
        there = pl.multiple_of(lax.rem(pos * (blocks // 2) + first + i, blocks) * tile, tile)
        here = slice(i * tile, i * tile + tile)
        data = split(jnp.concatenate([x_ref[pl.ds(there, tile), :], partner_ref[here, :]], 1))
        held[here, :] = dot_split(data, (high_ref[...], low_ref[...]))
        copies.append(
            pltpu.make_async_copy(held.at[here], out_ref.at[pl.ds(there, tile)], sems.at[i])
        )
        copies[-1].start()
    for copy in copies:
        copy.wait()


def apply(first, count, tile, snapshots, partner, high, low, out=None):
    rows, width = snapshots.shape
    extra = () if out is None else (out,)
    return pl.pallas_call(
        functools.partial(apply_kernel, first, count, tile),
        out_shape=jax.ShapeDtypeStruct((rows, width), jnp.float32),
        in_specs=[VMEM] * 4 + [ANY] * len(extra),
        out_specs=ANY,
        scratch_shapes=[
            pltpu.VMEM((count * tile, width), jnp.float32), pltpu.SemaphoreType.DMA((count,)),
        ],
        input_output_aliases={} if out is None else {4: 0},
        compiler_params=pltpu.CompilerParams(vmem_limit_bytes=24 * 1024 * 1024),
        cost_estimate=pl.CostEstimate(
            flops=count * tile * width * width * 48, bytes_accessed=count * tile * width * 16,
            transcendentals=0,
        ),
    )(snapshots, partner, high, low, *extra)


def pair_body(n, snapshots, grades, mover):
    rows, width = snapshots.shape
    share = width // n
    half = rows // 2
    piece = half // CHUNKS
    early = half + EXTRA * piece
    tile = TALL * piece
    f32 = jnp.float32
    dma = pltpu.SemaphoreType.DMA
    whole = pltpu.VMEM((2, n // 2, share, width), f32)
    part = pltpu.VMEM((n // 2, share, width), f32)
    one = pltpu.VMEM((share, width), f32)
    square = jax.ShapeDtypeStruct((width, width), f32)
    squares = jax.ShapeDtypeStruct((2, width, width), f32)
    diag, cross, turn, meta, near, late = pl.pallas_call(
        functools.partial(gram_kernel, n),
        out_shape=(
            squares, square, squares,
            jax.ShapeDtypeStruct((2, 8, width), f32),
            jax.ShapeDtypeStruct((early, width), f32),
            jax.ShapeDtypeStruct((rows - early, width), f32),
        ),
        in_specs=[VMEM, VMEM, pl.BlockSpec(memory_space=pltpu.SMEM)],
        out_specs=(VMEM, VMEM, VMEM, VMEM, VMEM, ANY),
        scratch_shapes=[
            pltpu.VMEM((8, width), f32), pltpu.VMEM((8, width), f32),
            whole, part, part, part, whole, whole,
            whole, part, part, part, one, one, whole,
            dma((CHUNKS + EXTRA,)), dma((CHUNKS + EXTRA,)),
            dma((2, n // 2)), dma((2, n // 2)), dma((2, n // 2)), dma((2, n // 2)),
            dma((4,)), dma((4,)), dma((3,)), dma((3,)),
            dma((2,)),
        ],
        compiler_params=pltpu.CompilerParams(
            collective_id=0, has_side_effects=True, vmem_limit_bytes=40 * 1024 * 1024
        ),
    )(snapshots, grades.reshape(1, width), mover)
    far = lax.ppermute(late, "blk", [(0, 1), (1, 0)])
    high, low = pl.pallas_call(
        chain_kernel,
        out_shape=(jax.ShapeDtypeStruct((2 * width, width), jnp.bfloat16),) * 2,
        in_specs=[VMEM] * 4,
        out_specs=(VMEM, VMEM),
        scratch_shapes=[
            pltpu.VMEM((16, BW, BW), f32),
            pltpu.VMEM((4, 2 * width, BW), f32),
            pltpu.VMEM((4, BW, BW), f32),
            pltpu.VMEM((4, 8, BW), f32),
        ],
        compiler_params=pltpu.CompilerParams(vmem_limit_bytes=32 * 1024 * 1024),
        cost_estimate=pl.CostEstimate(
            flops=15 * 10**9, bytes_accessed=4 * width * width * 8, transcendentals=0
        ),
    )(diag, cross, turn, meta)
    done = early // tile
    out = apply(0, done, tile, snapshots, near, high, low)
    return apply(done, rows // tile - done, tile, snapshots, far, high, low, out)


def solution(mesh):
    placed = (P("rows", "blk"), P("blk"), P(None, "blk"))
    n = mesh.shape["rows"]
    pairs = mesh.shape["blk"] == 2 and n % 2 == 0 and (2 * BW) % (8 * n) == 0
    body = functools.partial(pair_body, n) if pairs else general_body
    return jax.shard_map(
        body, mesh=mesh, in_specs=placed, out_specs=P("rows", "blk"), check_vma=False
    )
```
